256 devices in a mesh: ep: 4 (over x_hi, core), tp: 64 (over y, x_lo, z).
Axes of the slice: x: 4 (x_hi: 2, x_lo: 2; x = x_hi * 2 + x_lo), y: 4, z: 8, core: 2. Of those that a mesh axis runs over, the one named last changes fastest.
Arguments:
- tokens: bfloat16 [256, 3072], P(('ep', 'tp')), may hold values from -6 to 6
- cotangent: bfloat16 [256, 3072], P(('ep', 'tp')), may hold values from -6 to 6
- routes: int32 [256, 2], P(('ep', 'tp')), may hold values from 0 to 3, as said below
- gate_weights: bfloat16 [256, 2], P(('ep', 'tp')), may hold values from 0.099609375 to 1
- w_gate: bfloat16 [4, 3072, 8192], P('ep', None, 'tp'), may hold values from -0.109375 to 0.109375
- w_up: bfloat16 [4, 3072, 8192], P('ep', None, 'tp'), may hold values from -0.109375 to 0.109375
- w_down: bfloat16 [4, 8192, 3072], P('ep', 'tp'), may hold values from -0.0625 to 0.0625
Outputs:
- layer_out: bfloat16 [256, 3072], P(('ep', 'tp'))
- grad_tokens: bfloat16 [256, 3072], P(('ep', 'tp'))
- grad_gate: bfloat16 [4, 3072, 8192], P('ep', None, 'tp')
- grad_up: bfloat16 [4, 3072, 8192], P('ep', None, 'tp')
- grad_down: bfloat16 [4, 8192, 3072], P('ep', 'tp')
The draws below stay inside these ranges and needn't reach their ends.
Inputs may be any that keep to these rules, and one draw needn't show every extreme that they name: `routes`: each token names two different experts. One expert is named by exactly 224 tokens; every other expert by at most 107 tokens, and one of them by exactly 107.
All inputs are finite; a program needn't handle non-finite values.
Results may differ from the reference program's by a relative error of at most 0.005.
Values may be sent and summed in bfloat16 or wider, within the bound.
No kernel may reach another device: no remote copies, remote signals or barrier semaphores. Data moves between devices by JAX's collectives and lax.ppermute only.
A program may use at most 64 MiB of HBM per device.

```python
import jax
import jax.numpy as jnp

D = 3072
FF = 8192
EXPERTS = 4
TOKENS = 256
MOST = 224


def draw_routes(key, part):
    key_hot = jax.random.fold_in(key, 11)
    key_order = jax.random.fold_in(key, 12)
    key_others = jax.random.fold_in(key, 13)
    key_swap = jax.random.fold_in(key, 14)
    n_other = EXPERTS - 1
    hot_expert = jax.random.randint(key_hot, (), 0, EXPERTS).astype(jnp.int32)
    row_order = jax.random.permutation(key_order, TOKENS).astype(jnp.int32)
    position = jnp.zeros((TOKENS,), jnp.int32).at[row_order].set(jnp.arange(TOKENS, dtype=jnp.int32))
    other_order = jax.random.permutation(key_others, n_other).astype(jnp.int32)
    others = ((hot_expert + 1 + other_order) % EXPERTS).astype(jnp.int32)
    is_hot = position < MOST
    first = jnp.where(is_hot, hot_expert, others[0])
    second = jnp.where(is_hot, others[position % n_other], others[1 + position % (n_other - 1)])
    swapped = jax.random.randint(key_swap, (TOKENS,), 0, 2).astype(jnp.int32)
    column_a = jnp.where(swapped == 1, second, first)
    column_b = jnp.where(swapped == 1, first, second)
    return jnp.stack([column_a, column_b], axis=1).astype(jnp.int32)


def levels(stream_key, shape, cuts, low, high):
    loudness, own = 1.0, jax.random.fold_in(stream_key, 6)
    for dim, blocks in cuts:
        draws = jnp.exp(jax.random.uniform(jax.random.fold_in(own, dim), (blocks,), jnp.float32, low / len(cuts), high / len(cuts)))
        loudness = loudness * jnp.repeat(draws, shape[dim] // blocks).reshape([-1 if axis == dim else 1 for axis in range(len(shape))])
    return loudness


def centred(own_key, extent, width, reach, split=(), kind=jnp.bfloat16):
    array = jax.random.normal(own_key, extent, jnp.float32) * width
    if len(split) > 0:
        array = levels(own_key, extent, split, -0.22, 0.18) * array
    return jnp.clip(array, min=-reach, max=reach).astype(kind)


def setup_inputs(seed: int = 0) -> dict:
    keys = jax.random.split(jax.random.key(seed), 8)
    tokens = centred(keys[0], (TOKENS, D), 1.0, 6.0, ((0, 256),))
    cotangent = centred(keys[1], (TOKENS, D), 1.0, 6.0, ((0, 256),))
    routes = draw_routes(jax.random.fold_in(keys[7], 71), 0)
    gate_weights = jnp.clip(0.099609375 + 0.9003906 * jax.random.uniform(keys[3], (TOKENS, 2), jnp.float32) ** levels(keys[3], (TOKENS, 2), ((0, 256),), -0.2, 0.2), 0.099609375, 1.0).astype(jnp.bfloat16)
    w_gate = centred(keys[4], (EXPERTS, D, FF), D ** -0.5, 0.109375, ((0, 4), (2, 64)))
    w_up = centred(keys[5], (EXPERTS, D, FF), D ** -0.5, 0.109375, ((0, 4), (2, 64)))
    w_down = centred(keys[6], (EXPERTS, FF, D), FF ** -0.5, 0.0625, ((0, 4), (1, 64)))
    return dict(tokens=tokens, cotangent=cotangent, routes=routes, gate_weights=gate_weights, w_gate=w_gate, w_up=w_up, w_down=w_down)


def expert_pass(token_rows, cotan_rows, gate_column, gate_slice, up_slice, down_slice):
    gate_pre = jnp.dot(token_rows, gate_slice, preferred_element_type=jnp.float32)
    up_pre = jnp.dot(token_rows, up_slice, preferred_element_type=jnp.float32)
    sigmoid = jax.nn.sigmoid(gate_pre)
    silu_gate = gate_pre * sigmoid
    hidden = (silu_gate * up_pre * gate_column[:, None]).astype(jnp.bfloat16)
    output = jnp.dot(hidden, down_slice, preferred_element_type=jnp.float32)
    grad_hidden = jnp.dot(cotan_rows, down_slice.T, preferred_element_type=jnp.float32)
    grad_act = grad_hidden * gate_column[:, None]
    grad_gpre = (grad_act * up_pre * (sigmoid * (1.0 + gate_pre * (1.0 - sigmoid)))).astype(jnp.bfloat16)
    grad_upre = (grad_act * silu_gate).astype(jnp.bfloat16)
    grad_rows = jnp.dot(grad_gpre, gate_slice.T, preferred_element_type=jnp.float32) + jnp.dot(grad_upre, up_slice.T, preferred_element_type=jnp.float32)
    grad_gslice = jnp.dot(token_rows.T, grad_gpre, preferred_element_type=jnp.float32).astype(jnp.bfloat16)
    grad_uslice = jnp.dot(token_rows.T, grad_upre, preferred_element_type=jnp.float32).astype(jnp.bfloat16)
    grad_dslice = jnp.dot(hidden.T, cotan_rows, preferred_element_type=jnp.float32).astype(jnp.bfloat16)
    return output, grad_rows, grad_gslice, grad_uslice, grad_dslice


def reference(tokens, cotangent, routes, gate_weights, w_gate, w_up, w_down):
    expert_ids = jnp.arange(EXPERTS, dtype=jnp.int32)
    chosen = (routes[:, :, None] == expert_ids[None, None, :]).astype(jnp.float32)
    gate_table = jnp.sum(gate_weights.astype(jnp.float32)[:, :, None] * chosen, axis=1)
    total_out = jnp.zeros((TOKENS, D), jnp.float32)
    total_grad = jnp.zeros((TOKENS, D), jnp.float32)
    gate_grads = []
    up_grads = []
    down_grads = []
    for expert in range(EXPERTS):
        output, grad_rows, grad_gslice, grad_uslice, grad_dslice = expert_pass(tokens, cotangent, gate_table[:, expert], w_gate[expert], w_up[expert], w_down[expert])
        total_out = total_out + output
        total_grad = total_grad + grad_rows
        gate_grads.append(grad_gslice)
        up_grads.append(grad_uslice)
        down_grads.append(grad_dslice)
    return (total_out.astype(jnp.bfloat16), total_grad.astype(jnp.bfloat16), jnp.stack(gate_grads), jnp.stack(up_grads), jnp.stack(down_grads))
```

```python
import jax
import jax.numpy as jnp
from jax import lax
from jax.sharding import PartitionSpec as P

NX_HI, NCORE, NY, NX_LO, NZ = 2, 2, 4, 2, 8
NX = NX_HI * NX_LO
D = 3072
F32, BF16 = jnp.float32, jnp.bfloat16


def flat(x, core, y, z):
    return ((x // 2) * NCORE + core) * (NY * NX_LO * NZ) + (y * NX_LO + x % 2) * NZ + z


def pairs(axis, d):
    out = []
    for x in range(NX):
        for core in range(NCORE):
            for y in range(NY):
                for z in range(NZ):
                    to = dict(x=x, core=core, y=y, z=z)
                    size = dict(x=NX, core=NCORE, y=NY, z=NZ)[axis]
                    to[axis] = (to[axis] + d) % size
                    out.append((flat(x, core, y, z), flat(**to)))
    return out


def give(value, axis, d):
    return lax.ppermute(value, ("ep", "tp"), pairs(axis, d))


def fetch(value, axis, d):
    return lax.ppermute(value, ("ep", "tp"), pairs(axis, -d))


def contract(left, right, left_dim, right_dim):
    return lax.dot_general(
        left, right, (((left_dim,), (right_dim,)), ((), ())), preferred_element_type=F32
    )


def gathered(row_a, row_b):
    wide = row_a.shape[1]
    both = jnp.concatenate([row_a, row_b], axis=1)
    with jax.named_scope("gather_z"):
        eight = jnp.concatenate([both] + [fetch(both, "z", d) for d in range(1, NZ)], axis=0)
    a, b = eight[:, :wide], eight[:, wide:]
    with jax.named_scope("gather_first"):
        a = jnp.concatenate([a] + [fetch(a, "x", d) for d in range(1, NX)], axis=0)
        b = jnp.concatenate([b] + [fetch(b, "y", d) for d in range(1, NY)], axis=0)
    with jax.named_scope("gather_second"):
        a = jnp.concatenate([a] + [fetch(a, "y", d) for d in range(1, NY)], axis=0)
        parts = [b] + [fetch(b, "x", d) for d in range(1, NX)]
        b = jnp.stack([p.reshape(NY, NZ, -1) for p in parts], axis=1).reshape(NX * NY * NZ, -1)
    with jax.named_scope("gather_core"):
        return fetch(a, "core", 1), a, fetch(b, "core", 1), b


def reduced(out_far, out_near, grad_far, grad_near):
    with jax.named_scope("reduce_core"):
        a = out_near + give(out_far.astype(BF16), "core", 1).astype(F32)
        b = grad_near + give(grad_far.astype(BF16), "core", 1).astype(F32)
    with jax.named_scope("reduce_first"):
        a = a.reshape(NY, NX * NZ, D)
        b = b.reshape(NY, NX, NZ, D)
        got_a = [give(a[d].astype(BF16), "y", d) for d in range(1, NY)]
        got_b = [give(b[:, d].astype(BF16).reshape(NY * NZ, D), "x", d) for d in range(1, NX)]
        a = a[0] + sum(g.astype(F32) for g in got_a)
        b = b[:, 0].reshape(NY * NZ, D) + sum(g.astype(F32) for g in got_b)
    with jax.named_scope("reduce_second"):
        a = a.reshape(NX, NZ, D)
        b = b.reshape(NY, NZ, D)
        got_a = [give(a[d].astype(BF16), "x", d) for d in range(1, NX)]
        got_b = [give(b[d].astype(BF16), "y", d) for d in range(1, NY)]
        a = a[0] + sum(g.astype(F32) for g in got_a)
        b = b[0] + sum(g.astype(F32) for g in got_b)
    with jax.named_scope("reduce_z"):
        both = jnp.concatenate([a, b], axis=1)
        sent = both.astype(BF16)
        got = [give(sent[d : d + 1], "z", d) for d in range(1, NZ)]
        total = both[:1] + sum(g.astype(F32) for g in got)
    return total[:, :D].astype(BF16), total[:, D:].astype(BF16)


def on_device(tokens, cotangent, routes, gate_weights, w_gate, w_up, w_down):
    lane = lax.broadcasted_iota(jnp.int32, (1, 128), 1)
    weights = gate_weights.astype(F32)
    gates = jnp.where(routes[:, :1] == lane, weights[:, :1], 0.0) + jnp.where(
        routes[:, 1:] == lane, weights[:, 1:], 0.0
    )
    row_a = jnp.concatenate([tokens, gates.astype(BF16)], axis=1)
    a_far, a_near, b_far, b_near = gathered(row_a, cotangent)
    a = jnp.concatenate([a_far, a_near], axis=0)
    cot = jnp.concatenate([b_far, b_near], axis=0)
    x, gate_rows = a[:, :D], a[:, D:].astype(F32)
    own = lax.broadcasted_iota(jnp.int32, (1, 128), 1) == lax.axis_index("ep")
    column = jnp.sum(jnp.where(own, gate_rows, 0.0), axis=1, keepdims=True)
    gate_slice, up_slice, down_slice = w_gate[0], w_up[0], w_down[0]
    with jax.named_scope("experts"):
        gate_pre = contract(x, gate_slice, 1, 0)
        up_pre = contract(x, up_slice, 1, 0)
        sigmoid = jax.nn.sigmoid(gate_pre)
        silu = gate_pre * sigmoid
        hidden = (silu * up_pre * column).astype(BF16)
        output = contract(hidden, down_slice, 1, 0)
        grad_act = contract(cot, down_slice, 1, 1) * column
        grad_gpre = (grad_act * up_pre * (sigmoid * (1.0 + gate_pre * (1.0 - sigmoid)))).astype(BF16)
        grad_upre = (grad_act * silu).astype(BF16)
        grad_rows = contract(grad_gpre, gate_slice, 1, 1) + contract(grad_upre, up_slice, 1, 1)
        grad_g = contract(x, grad_gpre, 0, 0).astype(BF16)[None]
        grad_u = contract(x, grad_upre, 0, 0).astype(BF16)[None]
        grad_d = contract(hidden, cot, 0, 0).astype(BF16)[None]
    half = output.shape[0] // 2
    layer_out, grad_tokens = reduced(output[:half], output[half:], grad_rows[:half], grad_rows[half:])
    return layer_out, grad_tokens, grad_g, grad_u, grad_d


def solution(mesh):
    rows, columns, units = P(("ep", "tp"), None), P("ep", None, "tp"), P("ep", "tp", None)
    return jax.shard_map(
        on_device,
        mesh=mesh,
        in_specs=(rows, rows, rows, rows, columns, columns, units),
        out_specs=(rows, rows, columns, columns, units),
        check_vma=False,
    )
```

```python
import jax
import jax.numpy as jnp
from jax import lax
from jax.experimental import pallas as pl
from jax.experimental.pallas import tpu as pltpu
from jax.sharding import Mesh, PartitionSpec as P

NX_HI, NCORE, NY, NX_LO, NZ = 2, 2, 4, 2, 8
NXY = NX_HI * NX_LO * NY
AXES = ("x_hi", "core", "y", "x_lo", "z")
EP, TP, XY = ("x_hi", "core"), ("y", "x_lo", "z"), ("x_hi", "x_lo", "y")
D, PAD = 3072, 128
F32, BF16 = jnp.float32, jnp.bfloat16


def swapped(value):
    return lax.ppermute(value, "core", [(0, 1), (1, 0)])


def exchanged(value, axis):
    return lax.all_to_all(value, axis, 0, 0, tiled=True)


def contract(left, right, left_dim, right_dim):
    return lax.dot_general(
        left, right, (((left_dim,), (right_dim,)), ((), ())), preferred_element_type=F32
    )


def row_kernel(tokens, cotangent, routes, weights, out):
    lane = lax.broadcasted_iota(jnp.int32, (1, PAD), 1)
    r, w = routes[...], weights[...].astype(F32)
    gates = jnp.where(r[:, :1] == lane, w[:, :1], 0.0) + jnp.where(r[:, 1:] == lane, w[:, 1:], 0.0)
    first = jnp.concatenate([tokens[...].astype(F32), gates], axis=1)
    second = jnp.concatenate([cotangent[...].astype(F32), jnp.zeros((1, PAD), F32)], axis=1)
    both = jnp.concatenate([first, second], axis=0).astype(BF16)
    for i in range(NZ):
        out[i] = both


def copies_of_row(tokens, cotangent, routes, gate_weights):
    return pl.pallas_call(
        row_kernel,
        out_shape=jax.ShapeDtypeStruct((NZ, 2, D + PAD), BF16),
        name="copies_of_row",
    )(tokens, cotangent, routes, gate_weights)


def summed(parts):
    return sum(parts[i].astype(F32) for i in range(parts.shape[0]))


def on_device(tokens, cotangent, routes, gate_weights, w_gate, w_up, w_down):
    gate_slice, up_slice, down_slice = w_gate[0], w_up[0], w_down[0]
    half = NXY * NZ
    with jax.named_scope("gather_z"):
        eight = exchanged(copies_of_row(tokens, cotangent, routes, gate_weights), "z")
        eight = jnp.concatenate([eight[:, 0], eight[:, 1, :D]], axis=1)
    with jax.named_scope("gather_xy"):
        near = exchanged(jnp.broadcast_to(eight[None], (NXY,) + eight.shape), XY).reshape(half, -1)
    with jax.named_scope("gather_core"):
        rows = jnp.concatenate([swapped(near), near], axis=0)
    x, gate_rows, cot = rows[:, :D], rows[:, D : D + PAD].astype(F32), rows[:, D + PAD :]
    own = lax.broadcasted_iota(jnp.int32, (1, PAD), 1) == lax.axis_index(EP)
    column = jnp.sum(jnp.where(own, gate_rows, 0.0), axis=1, keepdims=True)
    with jax.named_scope("experts"):
        gate_pre = contract(x, gate_slice, 1, 0)
        up_pre = contract(x, up_slice, 1, 0)
        sigmoid = jax.nn.sigmoid(gate_pre)
        silu = gate_pre * sigmoid
        hidden = (silu * up_pre * column).astype(BF16)
        output = contract(hidden, down_slice, 1, 0)
        grad_act = contract(cot, down_slice, 1, 1) * column
        grad_gpre = (grad_act * up_pre * (sigmoid * (1.0 + gate_pre * (1.0 - sigmoid)))).astype(BF16)
        grad_upre = (grad_act * silu).astype(BF16)
        grad_rows = contract(grad_gpre, gate_slice, 1, 1) + contract(grad_upre, up_slice, 1, 1)
    with jax.named_scope("reduce_core"):
        out = output[half:] + swapped(output[:half].astype(BF16)).astype(F32)
        grad = grad_rows[half:] + swapped(grad_rows[:half].astype(BF16)).astype(F32)
    with jax.named_scope("reduce_xy"):
        both = jnp.concatenate([out.astype(BF16), grad.astype(BF16)], axis=1)
        both = summed(exchanged(both.reshape(NXY, NZ, 2 * D), XY)).astype(BF16)
    with jax.named_scope("weights"):
        grad_g = contract(x, grad_gpre, 0, 0).astype(BF16)[None]
        grad_u = contract(x, grad_upre, 0, 0).astype(BF16)[None]
        grad_d = contract(hidden, cot, 0, 0).astype(BF16)[None]
    with jax.named_scope("reduce_z"):
        total = summed(exchanged(both.reshape(NZ, 2, D), "z")).astype(BF16)
    return total[:1], total[1:], grad_g, grad_u, grad_d


def solution(mesh):
    fine = Mesh(mesh.devices.reshape(NX_HI, NCORE, NY, NX_LO, NZ), AXES)
    rows, columns, units = P(EP + TP, None), P(EP, None, TP), P(EP, TP, None)
    return jax.shard_map(
        on_device,
        mesh=fine,
        in_specs=(rows, rows, rows, rows, columns, columns, units),
        out_specs=(rows, rows, columns, columns, units),
        check_vma=False,
    )
```

```python
import jax
import jax.numpy as jnp
from jax import lax
from jax.experimental import pallas as pl
from jax.experimental.pallas import tpu as pltpu
from jax.sharding import Mesh, PartitionSpec as P

NX_HI, NCORE, NY, NX_LO, NZ, RING = 2, 2, 4, 2, 8, 4
AXES = ("x_hi", "core", "y", "x_lo", "z")
EP, TP = ("x_hi", "core"), ("y", "x_lo", "z")
D, PAD, UNITS = 3072, 128, 128
F32, BF16 = jnp.float32, jnp.bfloat16
VMEM = pl.BlockSpec(memory_space=pltpu.VMEM)
SMEM = pl.BlockSpec(memory_space=pltpu.SMEM)
PARAMS = pltpu.CompilerParams(vmem_limit_bytes=48 << 20)


def flat(x, core, y, z):
    return (((x // 2) * NCORE + core) * NY + y) * NX_LO * NZ + (x % 2) * NZ + z


def pairs(stage, d):
    out = []
    for x in range(RING):
        for core in range(NCORE):
            for y in range(RING):
                along_x = (stage == "light") == (core == 0)
                tx, ty = ((x + d) % RING, y) if along_x else (x, (y + d) % RING)
                out += [(flat(x, core, y, z), flat(tx, core, ty, z)) for z in range(NZ)]
    return out


def give(value, stage, d):
    return lax.ppermute(value, AXES, pairs(stage, d))


def fetch(value, stage, d):
    return lax.ppermute(value, AXES, pairs(stage, -d))


def swapped(value):
    return lax.ppermute(value, "core", [(0, 1), (1, 0)])


def exchanged(value, axis):
    return lax.all_to_all(value, axis, 0, 0, tiled=True)


def dot(left, right, left_dim, right_dim):
    return lax.dot_general(
        left, right, (((left_dim,), (right_dim,)), ((), ())), preferred_element_type=F32
    )


def row_kernel(tokens, cotangent, routes, weights, out):
    lane = lax.broadcasted_iota(jnp.int32, (1, PAD), 1)
    r, w = routes[...], weights[...].astype(F32)
    gates = jnp.where(r[:, :1] == lane, w[:, :1], 0.0) + jnp.where(r[:, 1:] == lane, w[:, 1:], 0.0)
    first = jnp.concatenate([tokens[...].astype(F32), gates], axis=1)
    second = jnp.concatenate([cotangent[...].astype(F32), jnp.zeros((1, PAD), F32)], axis=1)
    both = jnp.concatenate([first, second], axis=0).astype(BF16)
    for i in range(NZ):
        out[i] = both


def copies_of_row(tokens, cotangent, routes, gate_weights):
    return pl.pallas_call(
        row_kernel,
        out_shape=jax.ShapeDtypeStruct((NZ, 2, D + PAD), BF16),
        out_specs=VMEM,
        name="copies_of_row",
    )(tokens, cotangent, routes, gate_weights)


def expert_kernel(group, rows, gate_slice, up_slice, down_slice, terms, acts):
    lane = lax.broadcasted_iota(jnp.int32, (rows.shape[0], PAD), 1)
    gates = jnp.where(lane == group[0], rows[:, 2 * D :].astype(F32), 0.0)
    column = jnp.sum(gates, axis=1, keepdims=True)
    x, cot = rows[:, :D], rows[:, D : 2 * D]
    gate_pre = dot(x, gate_slice[...], 1, 0)
    up_pre = dot(x, up_slice[...], 1, 0)
    grad_act = dot(cot, down_slice[...], 1, 1) * column
    sigmoid = jax.nn.sigmoid(gate_pre)
    silu = gate_pre * sigmoid
    hidden = (silu * up_pre * column).astype(BF16)
    grad_gpre = (grad_act * up_pre * (sigmoid * (1.0 + gate_pre * (1.0 - sigmoid)))).astype(BF16)
    grad_upre = (grad_act * silu).astype(BF16)
    acts[:, :UNITS] = hidden
    acts[:, UNITS : 2 * UNITS] = grad_gpre
    acts[:, 2 * UNITS :] = grad_upre
    terms[:, :D] = dot(hidden, down_slice[...], 1, 0).astype(terms.dtype)
    grad_rows = dot(grad_gpre, gate_slice[...], 1, 1) + dot(grad_upre, up_slice[...], 1, 1)
    terms[:, D:] = grad_rows.astype(terms.dtype)


def expert_terms(group, rows, gate_slice, up_slice, down_slice, kind):
    n = rows.shape[0]
    return pl.pallas_call(
        expert_kernel,
        out_shape=(
            jax.ShapeDtypeStruct((n, 2 * D), kind),
            jax.ShapeDtypeStruct((n, 3 * UNITS), BF16),
        ),
        in_specs=[SMEM] + [VMEM] * 4,
        out_specs=(VMEM, VMEM),
        compiler_params=PARAMS,
        cost_estimate=pl.CostEstimate(
            flops=12 * n * D * UNITS, transcendentals=n * UNITS, bytes_accessed=4 * n * D + 6 * D * UNITS
        ),
        name="expert_terms",
    )(group, rows, gate_slice, up_slice, down_slice)


def weight_kernel(far, near, acts_far, acts_near, grad_g, grad_u, grad_d):
    u = UNITS

    def both(left_at, left_rows, right_at):
        def part(rows, acts):
            left = rows[:, left_at : left_at + D] if left_rows else acts[:, :u]
            right = acts[:, right_at : right_at + u] if left_rows else rows[:, D : 2 * D]
            return dot(left, right, 0, 0)

        return (part(far, acts_far) + part(near, acts_near)).astype(BF16)

    grad_g[0] = both(0, True, u)
    grad_u[0] = both(0, True, 2 * u)
    grad_d[0] = both(0, False, 0)


def weight_grads(far, near, acts_far, acts_near):
    n = 2 * far.shape[0]
    return pl.pallas_call(
        weight_kernel,
        out_shape=(
            jax.ShapeDtypeStruct((1, D, UNITS), BF16),
            jax.ShapeDtypeStruct((1, D, UNITS), BF16),
            jax.ShapeDtypeStruct((1, UNITS, D), BF16),
        ),
        in_specs=[VMEM] * 4,
        out_specs=(VMEM,) * 3,
        compiler_params=PARAMS,
        cost_estimate=pl.CostEstimate(
            flops=6 * n * D * UNITS, transcendentals=0, bytes_accessed=4 * n * D + 6 * D * UNITS
        ),
        name="weight_grads",
    )(far, near, acts_far, acts_near)


def last_kernel(own, one, two, three, out):
    total = own[...] + one[...].astype(F32) + two[...].astype(F32) + three[...].astype(F32)
    for i in range(NZ):
        row = total[i : i + 1]
        out[i] = jnp.concatenate([row[:, :D], row[:, D:]], axis=0).astype(BF16)


def summed_pairs(own, parts):
    return pl.pallas_call(
        last_kernel,
        out_shape=jax.ShapeDtypeStruct((NZ, 2, D), BF16),
        in_specs=[VMEM] * 4,
        out_specs=VMEM,
        name="summed_pairs",
    )(own, *parts)


def on_device(tokens, cotangent, routes, gate_weights, w_gate, w_up, w_down):
    slices = (w_gate[0], w_up[0], w_down[0])
    group = lax.axis_index(EP).astype(jnp.int32).reshape(1)
    with jax.named_scope("gather_z"):
        rows = exchanged(copies_of_row(tokens, cotangent, routes, gate_weights), "z")
        rows = jnp.concatenate([rows[:, 0, :D], rows[:, 1, :D], rows[:, 0, D:]], axis=1)
    with jax.named_scope("gather_light"):
        rows = jnp.concatenate([rows] + [fetch(rows, "light", d) for d in range(1, RING)], axis=0)
    with jax.named_scope("gather_heavy"):
        near = [rows] + [fetch(rows, "heavy", d) for d in range(1, RING)]
    with jax.named_scope("gather_core"):
        far = jnp.concatenate([swapped(chunk) for chunk in near], axis=0)
        near = jnp.concatenate(near, axis=0)
    with jax.named_scope("experts"):
        far_terms, far_acts = expert_terms(group, far, *slices, BF16)
        other = swapped(far_terms)
        near_terms, near_acts = expert_terms(group, near, *slices, F32)
    with jax.named_scope("weights"):
        grad_g, grad_u, grad_d = weight_grads(far, near, far_acts, near_acts)
    with jax.named_scope("reduce_heavy"):
        total = (near_terms + other.astype(F32)).reshape(RING, RING * NZ, 2 * D)
        got = [give(total[d].astype(BF16), "heavy", d) for d in range(1, RING)]
        total = total[0] + sum(g.astype(F32) for g in got)
    with jax.named_scope("reduce_light"):
        total = total.reshape(RING, NZ, 2 * D)
        got = [give(total[d].astype(BF16), "light", d) for d in range(1, RING)]
    with jax.named_scope("reduce_z"):
        got = exchanged(summed_pairs(total[0], got), "z")
        total = sum(got[i].astype(F32) for i in range(NZ)).astype(BF16)
    return total[:1], total[1:], grad_g, grad_u, grad_d


def solution(mesh):
    fine = Mesh(mesh.devices.reshape(NX_HI, NCORE, NY, NX_LO, NZ), AXES)
    rows, columns, units = P(EP + TP, None), P(EP, None, TP), P(EP, TP, None)
    return jax.shard_map(
        on_device,
        mesh=fine,
        in_specs=(rows, rows, rows, rows, columns, columns, units),
        out_specs=(rows, rows, columns, columns, units),
        check_vma=False,
    )
```

```python
import jax
import jax.numpy as jnp
from jax import lax
from jax.experimental import pallas as pl
from jax.experimental.pallas import tpu as pltpu
from jax.sharding import Mesh, PartitionSpec as P

NX_HI, NCORE, NY, NX_LO, NZ, RING = 2, 2, 4, 2, 8, 4
AXES = ("x_hi", "core", "y", "x_lo", "z")
EP, TP = ("x_hi", "core"), ("y", "x_lo", "z")
D, PAD, UNITS = 3072, 128, 128
F32, BF16 = jnp.float32, jnp.bfloat16
VMEM = pl.BlockSpec(memory_space=pltpu.VMEM)
SMEM = pl.BlockSpec(memory_space=pltpu.SMEM)


def grant(mebibytes):
    return pltpu.CompilerParams(vmem_limit_bytes=mebibytes << 20)


def flat(x, core, y, z):
    return (((x // 2) * NCORE + core) * NY + y) * NX_LO * NZ + (x % 2) * NZ + z


def pairs(stage, kind):
    mate = (lambda p: p ^ 1) if kind == "low" else (lambda p: 3 - p)
    out = []
    for x in range(RING):
        for core in range(NCORE):
            for y in range(RING):
                along_x = (stage == "light") == (core == 0)
                tx, ty = (mate(x), y) if along_x else (x, mate(y))
                out += [(flat(x, core, y, z), flat(tx, core, ty, z)) for z in range(NZ)]
    return out


def mated(value, stage, kind):
    return lax.ppermute(value, AXES, pairs(stage, kind))


def swapped(value):
    return lax.ppermute(value, "core", [(0, 1), (1, 0)])


def exchanged(value, axis):
    return lax.all_to_all(value, axis, 0, 0, tiled=True)


def dot(left, right, left_dim, right_dim):
    return lax.dot_general(
        left, right, (((left_dim,), (right_dim,)), ((), ())), preferred_element_type=F32
    )


def row_kernel(tokens, cotangent, routes, weights, out):
    lane = lax.broadcasted_iota(jnp.int32, (1, PAD), 1)
    r, w = routes[...], weights[...].astype(F32)
    gates = jnp.where(r[:, :1] == lane, w[:, :1], 0.0) + jnp.where(r[:, 1:] == lane, w[:, 1:], 0.0)
    first = jnp.concatenate([tokens[...].astype(F32), gates], axis=1)
    second = jnp.concatenate([cotangent[...].astype(F32), jnp.zeros((1, PAD), F32)], axis=1)
    both = jnp.concatenate([first, second], axis=0).astype(BF16)
    for i in range(NZ):
        out[i] = both


def copies_of_row(tokens, cotangent, routes, gate_weights):
    return pl.pallas_call(
        row_kernel,
        out_shape=jax.ShapeDtypeStruct((NZ, 2, D + PAD), BF16),
        out_specs=VMEM,
        name="copies_of_row",
    )(tokens, cotangent, routes, gate_weights)


def other_order(value):
    blocks = []
    for k in range(RING * RING):
        h1, h0, l1, l0 = (k >> 3) & 1, (k >> 2) & 1, (k >> 1) & 1, k & 1
        at = (h0 * 8 + h1 * 4 + l0 * 2 + l1) * NZ
        blocks.append(value[at : at + NZ])
    return jnp.concatenate(blocks, axis=0)


def expert_kernel(group, rows, cot, gate_slice, up_slice, down_slice, out, grad, acts):
    lane = lax.broadcasted_iota(jnp.int32, (rows.shape[0], PAD), 1)
    gates = jnp.where(lane == group[0], rows[:, D:].astype(F32), 0.0)
    column = jnp.sum(gates, axis=1, keepdims=True)
    x = rows[:, :D]
    gate_pre = dot(x, gate_slice[...], 1, 0)
    up_pre = dot(x, up_slice[...], 1, 0)
    grad_act = other_order(dot(cot[...], down_slice[...], 1, 1)) * column
    sigmoid = jax.nn.sigmoid(gate_pre)
    silu = gate_pre * sigmoid
    hidden = silu * up_pre * column
    grad_gpre = grad_act * up_pre * (sigmoid * (1.0 + gate_pre * (1.0 - sigmoid)))
    grad_upre = grad_act * silu
    acts[:, :UNITS] = other_order(hidden).astype(BF16)
    acts[:, UNITS : 2 * UNITS] = grad_gpre.astype(BF16)
    acts[:, 2 * UNITS :] = grad_upre.astype(BF16)
    out[...] = dot(hidden.astype(BF16), down_slice[...], 1, 0).astype(out.dtype)
    grad_rows = dot(other_order(grad_gpre).astype(BF16), gate_slice[...], 1, 1)
    grad_rows += dot(other_order(grad_upre).astype(BF16), up_slice[...], 1, 1)
    grad[...] = grad_rows.astype(grad.dtype)


def expert_terms(group, rows, cot, gate_slice, up_slice, down_slice, kind):
    n = rows.shape[0]
    return pl.pallas_call(
        expert_kernel,
        out_shape=(
            jax.ShapeDtypeStruct((n, D), kind),
            jax.ShapeDtypeStruct((n, D), kind),
            jax.ShapeDtypeStruct((n, 3 * UNITS), BF16),
        ),
        in_specs=[SMEM] + [VMEM] * 5,
        out_specs=(VMEM,) * 3,
        compiler_params=grant(16),
        cost_estimate=pl.CostEstimate(
            flops=12 * n * D * UNITS, transcendentals=n * UNITS, bytes_accessed=4 * n * D + 6 * D * UNITS
        ),
        name="expert_terms",
    )(group, rows, cot, gate_slice, up_slice, down_slice)


def weight_kernel(far, near, cot_far, cot_near, acts_far, acts_near, grad_g, grad_u, grad_d):
    u = UNITS
    for grad, at in ((grad_g, u), (grad_u, 2 * u)):
        total = dot(far[:, :D], acts_far[:, at : at + u], 0, 0)
        total += dot(near[:, :D], acts_near[:, at : at + u], 0, 0)
        grad[0] = total.astype(BF16)
    total = dot(acts_far[:, :u], cot_far[...], 0, 0) + dot(acts_near[:, :u], cot_near[...], 0, 0)
    grad_d[0] = total.astype(BF16)


def weight_grads(*operands):
    n = 2 * operands[0].shape[0]
    return pl.pallas_call(
        weight_kernel,
        out_shape=(
            jax.ShapeDtypeStruct((1, D, UNITS), BF16),
            jax.ShapeDtypeStruct((1, D, UNITS), BF16),
            jax.ShapeDtypeStruct((1, UNITS, D), BF16),
        ),
        in_specs=[VMEM] * 6,
        out_specs=(VMEM,) * 3,
        compiler_params=grant(16),
        cost_estimate=pl.CostEstimate(
            flops=6 * n * D * UNITS, transcendentals=0, bytes_accessed=4 * n * D + 6 * D * UNITS
        ),
        name="weight_grads",
    )(*operands)


def last_kernel(own_a, got_a, own_b, got_b, out):
    a = own_a[...] + got_a[...].astype(F32)
    b = own_b[...] + got_b[...].astype(F32)
    for i in range(NZ):
        out[i] = jnp.concatenate([a[i : i + 1], b[i : i + 1]], axis=0).astype(BF16)


def summed_pairs(*operands):
    return pl.pallas_call(
        last_kernel,
        out_shape=jax.ShapeDtypeStruct((NZ, 2, D), BF16),
        in_specs=[VMEM] * 4,
        out_specs=VMEM,
        compiler_params=grant(1),
        name="summed_pairs",
    )(*operands)


def doubled(a, b, stage):
    for kind_a, kind_b in (("low", "high"), ("high", "low")):
        got_a, got_b = mated(a, stage, kind_a), mated(b, stage, kind_b)
        a, b = jnp.concatenate([a, got_a], axis=0), jnp.concatenate([b, got_b], axis=0)
    return a, b


def halves(value):
    n = value.shape[0] // 2
    return value[:n], value[n:].astype(BF16)


def on_device(tokens, cotangent, routes, gate_weights, w_gate, w_up, w_down):
    slices = (w_gate[0], w_up[0], w_down[0])
    group = lax.axis_index(EP).astype(jnp.int32).reshape(1)
    with jax.named_scope("gather_z"):
        rows = exchanged(copies_of_row(tokens, cotangent, routes, gate_weights), "z")
        a, b = rows[:, 0], rows[:, 1, :D]
    with jax.named_scope("gather_light"):
        a, b = doubled(a, b, "light")
    with jax.named_scope("gather_heavy"):
        a, b = doubled(a, b, "heavy")
    with jax.named_scope("gather_core"):
        n = a.shape[0] // 2
        far_a = jnp.concatenate([swapped(a[:n]), swapped(a[n:])], axis=0)
        far_b = jnp.concatenate([swapped(b[:n]), swapped(b[n:])], axis=0)
    with jax.named_scope("experts"):
        far_out, far_grad, far_acts = expert_terms(group, far_a, far_b, *slices, BF16)
        other_out, other_grad = swapped(far_out), swapped(far_grad)
        near_out, near_grad, near_acts = expert_terms(group, a, b, *slices, F32)
    with jax.named_scope("weights"):
        grad_g, grad_u, grad_d = weight_grads(far_a, a, far_b, b, far_acts, near_acts)
    out, grad = near_out + other_out.astype(F32), near_grad + other_grad.astype(F32)
    steps = [(stage, kind) for stage in ("heavy", "light") for kind in ("high", "low")]
    for stage, kind in steps:
        with jax.named_scope("reduce_" + stage):
            (out, send_out), (grad, send_grad) = halves(out), halves(grad)
            got_out = mated(send_out, stage, kind)
            got_grad = mated(send_grad, stage, "low" if kind == "high" else "high")
            if (stage, kind) != steps[-1]:
                out, grad = out + got_out.astype(F32), grad + got_grad.astype(F32)
    with jax.named_scope("reduce_z"):
        got = exchanged(summed_pairs(out, got_out, grad, got_grad), "z")
        total = sum(got[i].astype(F32) for i in range(NZ)).astype(BF16)
    return total[:1], total[1:], grad_g, grad_u, grad_d


def solution(mesh):
    fine = Mesh(mesh.devices.reshape(NX_HI, NCORE, NY, NX_LO, NZ), AXES)
    rows, columns, units = P(EP + TP, None), P(EP, None, TP), P(EP, TP, None)
    return jax.shard_map(
        on_device,
        mesh=fine,
        in_specs=(rows, rows, rows, rows, columns, columns, units),
        out_specs=(rows, rows, columns, columns, units),
        check_vma=False,
    )
```

```python
import jax
import jax.numpy as jnp
from jax import lax
from jax.experimental import pallas as pl
from jax.experimental.pallas import tpu as pltpu
from jax.sharding import Mesh, PartitionSpec as P

NX_HI, NCORE, NY, NX_LO, NZ, RING = 2, 2, 4, 2, 8, 4
AXES = ("x_hi", "core", "y", "x_lo", "z")
EP, TP = ("x_hi", "core"), ("y", "x_lo", "z")
D, PAD, UNITS = 3072, 128, 128
F32, BF16 = jnp.float32, jnp.bfloat16
VMEM = pl.BlockSpec(memory_space=pltpu.VMEM)
SMEM = pl.BlockSpec(memory_space=pltpu.SMEM)
ORDER = (2, 1, 3)


def grant(mebibytes):
    return pltpu.CompilerParams(vmem_limit_bytes=mebibytes << 20)


def flat(x, core, y, z):
    return (((x // 2) * NCORE + core) * NY + y) * NX_LO * NZ + (x % 2) * NZ + z


def pairs(stage, d):
    out = []
    for x in range(RING):
        for core in range(NCORE):
            for y in range(RING):
                along_x = (stage == "light") == (core == 0)
                tx, ty = ((x + d) % RING, y) if along_x else (x, (y + d) % RING)
                out += [(flat(x, core, y, z), flat(tx, core, ty, z)) for z in range(NZ)]
    return out


def give(value, stage, d):
    return lax.ppermute(value, AXES, pairs(stage, d))


def fetch(value, stage, d):
    return lax.ppermute(value, AXES, pairs(stage, -d))


def swapped(value):
    return lax.ppermute(value, "core", [(0, 1), (1, 0)])


def exchanged(value, axis):
    return lax.all_to_all(value, axis, 0, 0, tiled=True)


def dot(left, right, left_dim, right_dim):
    return lax.dot_general(
        left, right, (((left_dim,), (right_dim,)), ((), ())), preferred_element_type=F32
    )


def row_kernel(tokens, cotangent, routes, weights, out):
    lane = lax.broadcasted_iota(jnp.int32, (1, PAD), 1)
    r, w = routes[...], weights[...].astype(F32)
    gates = jnp.where(r[:, :1] == lane, w[:, :1], 0.0) + jnp.where(r[:, 1:] == lane, w[:, 1:], 0.0)
    first = jnp.concatenate([tokens[...].astype(F32), gates], axis=1)
    second = jnp.concatenate([cotangent[...].astype(F32), jnp.zeros((1, PAD), F32)], axis=1)
    both = jnp.concatenate([first, second], axis=0).astype(BF16)
    for i in range(NZ):
        out[i] = both


def copies_of_row(tokens, cotangent, routes, gate_weights):
    return pl.pallas_call(
        row_kernel,
        out_shape=jax.ShapeDtypeStruct((NZ, 2, D + PAD), BF16),
        out_specs=VMEM,
        name="copies_of_row",
    )(tokens, cotangent, routes, gate_weights)


def expert_kernel(group, rows, gate_slice, up_slice, down_slice, terms, acts):
    lane = lax.broadcasted_iota(jnp.int32, (rows.shape[0], PAD), 1)
    gates = jnp.where(lane == group[0], rows[:, 2 * D :].astype(F32), 0.0)
    column = jnp.sum(gates, axis=1, keepdims=True)
    x, cot = rows[:, :D], rows[:, D : 2 * D]
    gate_pre = dot(x, gate_slice[...], 1, 0)
    up_pre = dot(x, up_slice[...], 1, 0)
    grad_act = dot(cot, down_slice[...], 1, 1) * column
    sigmoid = jax.nn.sigmoid(gate_pre)
    silu = gate_pre * sigmoid
    hidden = (silu * up_pre * column).astype(BF16)
    grad_gpre = (grad_act * up_pre * (sigmoid * (1.0 + gate_pre * (1.0 - sigmoid)))).astype(BF16)
    grad_upre = (grad_act * silu).astype(BF16)
    acts[:, :UNITS] = hidden
    acts[:, UNITS : 2 * UNITS] = grad_gpre
    acts[:, 2 * UNITS :] = grad_upre
    terms[:, :D] = dot(hidden, down_slice[...], 1, 0).astype(terms.dtype)
    grad_rows = dot(grad_gpre, gate_slice[...], 1, 1) + dot(grad_upre, up_slice[...], 1, 1)
    terms[:, D:] = grad_rows.astype(terms.dtype)


def expert_terms(group, rows, gate_slice, up_slice, down_slice, kind):
    n = rows.shape[0]
    return pl.pallas_call(
        expert_kernel,
        out_shape=(
            jax.ShapeDtypeStruct((n, 2 * D), kind),
            jax.ShapeDtypeStruct((n, 3 * UNITS), BF16),
        ),
        in_specs=[SMEM] + [VMEM] * 4,
        out_specs=(VMEM, VMEM),
        compiler_params=grant(16),
        cost_estimate=pl.CostEstimate(
            flops=12 * n * D * UNITS, transcendentals=n * UNITS, bytes_accessed=4 * n * D + 6 * D * UNITS
        ),
        name="expert_terms",
    )(group, rows, gate_slice, up_slice, down_slice)


def weight_kernel(far, near, acts_far, acts_near, grad_g, grad_u, grad_d):
    u = UNITS

    def both(left_at, left_rows, right_at):
        def part(rows, acts):
            left = rows[:, left_at : left_at + D] if left_rows else acts[:, :u]
            right = acts[:, right_at : right_at + u] if left_rows else rows[:, D : 2 * D]
            return dot(left, right, 0, 0)

        return (part(far, acts_far) + part(near, acts_near)).astype(BF16)

    grad_g[0] = both(0, True, u)
    grad_u[0] = both(0, True, 2 * u)
    grad_d[0] = both(0, False, 0)


def weight_grads(far, near, acts_far, acts_near):
    n = 2 * far.shape[0]
    return pl.pallas_call(
        weight_kernel,
        out_shape=(
            jax.ShapeDtypeStruct((1, D, UNITS), BF16),
            jax.ShapeDtypeStruct((1, D, UNITS), BF16),
            jax.ShapeDtypeStruct((1, UNITS, D), BF16),
        ),
        in_specs=[VMEM] * 4,
        out_specs=(VMEM,) * 3,
        compiler_params=grant(16),
        cost_estimate=pl.CostEstimate(
            flops=6 * n * D * UNITS, transcendentals=0, bytes_accessed=4 * n * D + 6 * D * UNITS
        ),
        name="weight_grads",
    )(far, near, acts_far, acts_near)


def last_kernel(own, one, two, three, out):
    total = own[...] + one[...].astype(F32) + two[...].astype(F32) + three[...].astype(F32)
    for i in range(NZ):
        row = total[i : i + 1]
        out[i] = jnp.concatenate([row[:, :D], row[:, D:]], axis=0).astype(BF16)


def summed_pairs(own, parts):
    return pl.pallas_call(
        last_kernel,
        out_shape=jax.ShapeDtypeStruct((NZ, 2, D), BF16),
        in_specs=[VMEM] * 4,
        out_specs=VMEM,
        compiler_params=grant(1),
        name="summed_pairs",
    )(own, *parts)


def on_device(tokens, cotangent, routes, gate_weights, w_gate, w_up, w_down):
    slices = (w_gate[0], w_up[0], w_down[0])
    group = lax.axis_index(EP).astype(jnp.int32).reshape(1)
    with jax.named_scope("gather_z"):
        rows = exchanged(copies_of_row(tokens, cotangent, routes, gate_weights), "z")
        rows = jnp.concatenate([rows[:, 0, :D], rows[:, 1, :D], rows[:, 0, D:]], axis=1)
    with jax.named_scope("gather_light"):
        rows = jnp.concatenate([rows] + [fetch(rows, "light", d) for d in ORDER], axis=0)
    with jax.named_scope("gather_heavy"):
        near = [rows] + [fetch(rows, "heavy", d) for d in ORDER]
    with jax.named_scope("gather_core"):
        far = jnp.concatenate([swapped(chunk) for chunk in near], axis=0)
        near = jnp.concatenate(near, axis=0)
    with jax.named_scope("experts"):
        far_terms, far_acts = expert_terms(group, far, *slices, BF16)
        other = swapped(far_terms)
        near_terms, near_acts = expert_terms(group, near, *slices, F32)
    with jax.named_scope("weights"):
        grad_g, grad_u, grad_d = weight_grads(far, near, far_acts, near_acts)
    with jax.named_scope("reduce_heavy"):
        total = (near_terms + other.astype(F32)).reshape(RING, RING * NZ, 2 * D)
        got = [give(total[1 + i].astype(BF16), "heavy", d) for i, d in enumerate(ORDER)]
        total = total[0] + sum(g.astype(F32) for g in got)
    with jax.named_scope("reduce_light"):
        total = total.reshape(RING, NZ, 2 * D)
        got = [give(total[1 + i].astype(BF16), "light", d) for i, d in enumerate(ORDER)]
    with jax.named_scope("reduce_z"):
        got = exchanged(summed_pairs(total[0], got), "z")
        total = sum(got[i].astype(F32) for i in range(NZ)).astype(BF16)
    return total[:1], total[1:], grad_g, grad_u, grad_d


def solution(mesh):
    fine = Mesh(mesh.devices.reshape(NX_HI, NCORE, NY, NX_LO, NZ), AXES)
    rows, columns, units = P(EP + TP, None), P(EP, None, TP), P(EP, TP, None)
    return jax.shard_map(
        on_device,
        mesh=fine,
        in_specs=(rows, rows, rows, rows, columns, columns, units),
        out_specs=(rows, rows, columns, columns, units),
        check_vma=False,
    )
```

```python
import jax
import jax.numpy as jnp
from jax import lax
from jax.experimental import pallas as pl
from jax.experimental.pallas import tpu as pltpu
from jax.sharding import Mesh, PartitionSpec as P

NX_HI, NCORE, NY, NX_LO, NZ, RING, PLANE = 2, 2, 4, 2, 8, 4, 32
AXES = ("x_hi", "core", "y", "x_lo", "z")
EP, TP = ("x_hi", "core"), ("y", "x_lo", "z")
D, PAD, UNITS = 3072, 128, 128
F32, BF16 = jnp.float32, jnp.bfloat16
VMEM = pl.BlockSpec(memory_space=pltpu.VMEM)
SMEM = pl.BlockSpec(memory_space=pltpu.SMEM)
ORDER = (2, 1, 3)


def grant(mebibytes):
    return pltpu.CompilerParams(vmem_limit_bytes=mebibytes << 20)


def flat(x, core, y, z):
    return (((x // 2) * NCORE + core) * NY + y) * NX_LO * NZ + (x % 2) * NZ + z


def pairs(d):
    out = []
    for x in range(RING):
        for core in range(NCORE):
            for y in range(RING):
                tx, ty = (x, (y + d) % RING) if core == 0 else ((x + d) % RING, y)
                out += [(flat(x, core, y, z), flat(tx, core, ty, z)) for z in range(NZ)]
    return out


def give(value, d):
    return lax.ppermute(value, AXES, pairs(d))


def fetch(value, d):
    return lax.ppermute(value, AXES, pairs(-d))


def swapped(value):
    return lax.ppermute(value, "core", [(0, 1), (1, 0)])


def planes():
    along_x = [[flat(x, 0, y, z) for x in range(RING) for z in range(NZ)] for y in range(RING)]
    along_y = [[flat(x, 1, y, z) for y in range(RING) for z in range(NZ)] for x in range(RING)]
    return along_x + along_y


def exchanged(value):
    return lax.all_to_all(value, AXES, 0, 0, axis_index_groups=planes(), tiled=True)


def dot(left, right, left_dim, right_dim):
    return lax.dot_general(
        left, right, (((left_dim,), (right_dim,)), ((), ())), preferred_element_type=F32
    )


def row_kernel(tokens, cotangent, routes, weights, out):
    lane = lax.broadcasted_iota(jnp.int32, (1, PAD), 1)
    r, w = routes[...], weights[...].astype(F32)
    gates = jnp.where(r[:, :1] == lane, w[:, :1], 0.0) + jnp.where(r[:, 1:] == lane, w[:, 1:], 0.0)
    first = jnp.concatenate([tokens[...].astype(F32), gates], axis=1)
    second = jnp.concatenate([cotangent[...].astype(F32), jnp.zeros((1, PAD), F32)], axis=1)
    both = jnp.concatenate([first, second], axis=0).astype(BF16)
    for i in range(PLANE):
        out[i] = both


def copies_of_row(tokens, cotangent, routes, gate_weights):
    return pl.pallas_call(
        row_kernel,
        out_shape=jax.ShapeDtypeStruct((PLANE, 2, D + PAD), BF16),
        out_specs=VMEM,
        name="copies_of_row",
    )(tokens, cotangent, routes, gate_weights)


def expert_kernel(group, rows, gate_slice, up_slice, down_slice, terms, acts):
    lane = lax.broadcasted_iota(jnp.int32, (rows.shape[0], PAD), 1)
    gates = jnp.where(lane == group[0], rows[:, 2 * D :].astype(F32), 0.0)
    column = jnp.sum(gates, axis=1, keepdims=True)
    x, cot = rows[:, :D], rows[:, D : 2 * D]
    gate_pre = dot(x, gate_slice[...], 1, 0)
    up_pre = dot(x, up_slice[...], 1, 0)
    grad_act = dot(cot, down_slice[...], 1, 1) * column
    sigmoid = jax.nn.sigmoid(gate_pre)
    silu = gate_pre * sigmoid
    hidden = (silu * up_pre * column).astype(BF16)
    grad_gpre = (grad_act * up_pre * (sigmoid * (1.0 + gate_pre * (1.0 - sigmoid)))).astype(BF16)
    grad_upre = (grad_act * silu).astype(BF16)
    acts[:, :UNITS] = hidden
    acts[:, UNITS : 2 * UNITS] = grad_gpre
    acts[:, 2 * UNITS :] = grad_upre
    terms[:, :D] = dot(hidden, down_slice[...], 1, 0).astype(terms.dtype)
    grad_rows = dot(grad_gpre, gate_slice[...], 1, 1) + dot(grad_upre, up_slice[...], 1, 1)
    terms[:, D:] = grad_rows.astype(terms.dtype)


def expert_terms(group, rows, gate_slice, up_slice, down_slice, kind):
    n = rows.shape[0]
    return pl.pallas_call(
        expert_kernel,
        out_shape=(
            jax.ShapeDtypeStruct((n, 2 * D), kind),
            jax.ShapeDtypeStruct((n, 3 * UNITS), BF16),
        ),
        in_specs=[SMEM] + [VMEM] * 4,
        out_specs=(VMEM, VMEM),
        compiler_params=grant(16),
        cost_estimate=pl.CostEstimate(
            flops=12 * n * D * UNITS, transcendentals=n * UNITS, bytes_accessed=4 * n * D + 6 * D * UNITS
        ),
        name="expert_terms",
    )(group, rows, gate_slice, up_slice, down_slice)


def weight_kernel(far, near, acts_far, acts_near, grad_g, grad_u, grad_d):
    u = UNITS

    def both(left_at, left_rows, right_at):
        def part(rows, acts):
            left = rows[:, left_at : left_at + D] if left_rows else acts[:, :u]
            right = acts[:, right_at : right_at + u] if left_rows else rows[:, D : 2 * D]
            return dot(left, right, 0, 0)

        return (part(far, acts_far) + part(near, acts_near)).astype(BF16)

    grad_g[0] = both(0, True, u)
    grad_u[0] = both(0, True, 2 * u)
    grad_d[0] = both(0, False, 0)


def weight_grads(far, near, acts_far, acts_near):
    n = 2 * far.shape[0]
    return pl.pallas_call(
        weight_kernel,
        out_shape=(
            jax.ShapeDtypeStruct((1, D, UNITS), BF16),
            jax.ShapeDtypeStruct((1, D, UNITS), BF16),
            jax.ShapeDtypeStruct((1, UNITS, D), BF16),
        ),
        in_specs=[VMEM] * 4,
        out_specs=(VMEM,) * 3,
        compiler_params=grant(16),
        cost_estimate=pl.CostEstimate(
            flops=6 * n * D * UNITS, transcendentals=0, bytes_accessed=4 * n * D + 6 * D * UNITS
        ),
        name="weight_grads",
    )(far, near, acts_far, acts_near)


def last_kernel(own, one, two, three, out):
    total = own[...] + one[...].astype(F32) + two[...].astype(F32) + three[...].astype(F32)
    for i in range(PLANE):
        row = total[i : i + 1]
        out[i] = jnp.concatenate([row[:, :D], row[:, D:]], axis=0).astype(BF16)


def summed_pairs(own, parts):
    return pl.pallas_call(
        last_kernel,
        out_shape=jax.ShapeDtypeStruct((PLANE, 2, D), BF16),
        in_specs=[VMEM] * 4,
        out_specs=VMEM,
        compiler_params=grant(4),
        name="summed_pairs",
    )(own, *parts)


def on_device(tokens, cotangent, routes, gate_weights, w_gate, w_up, w_down):
    slices = (w_gate[0], w_up[0], w_down[0])
    group = lax.axis_index(EP).astype(jnp.int32).reshape(1)
    with jax.named_scope("gather_plane"):
        rows = exchanged(copies_of_row(tokens, cotangent, routes, gate_weights))
        rows = jnp.concatenate([rows[:, 0, :D], rows[:, 1, :D], rows[:, 0, D:]], axis=1)
    with jax.named_scope("gather_heavy"):
        near = [rows] + [fetch(rows, d) for d in ORDER]
    with jax.named_scope("gather_core"):
        far = jnp.concatenate([swapped(chunk) for chunk in near], axis=0)
        far, near = lax.optimization_barrier((far, jnp.concatenate(near, axis=0)))
    with jax.named_scope("experts"):
        far_terms, far_acts = expert_terms(group, far, *slices, BF16)
        other = swapped(far_terms)
        near_terms, near_acts = expert_terms(group, near, *slices, F32)
    with jax.named_scope("weights"):
        grad_g, grad_u, grad_d = weight_grads(far, near, far_acts, near_acts)
    with jax.named_scope("reduce_heavy"):
        total = (near_terms + other.astype(F32)).reshape(RING, PLANE, 2 * D)
        got = [give(total[1 + i].astype(BF16), d) for i, d in enumerate(ORDER)]
    with jax.named_scope("reduce_plane"):
        got = exchanged(summed_pairs(total[0], got))
        total = sum(got[i].astype(F32) for i in range(PLANE)).astype(BF16)
    return total[:1], total[1:], grad_g, grad_u, grad_d


def solution(mesh):
    fine = Mesh(mesh.devices.reshape(NX_HI, NCORE, NY, NX_LO, NZ), AXES)
    rows, columns, units = P(EP + TP, None), P(EP, None, TP), P(EP, TP, None)
    return jax.shard_map(
        on_device,
        mesh=fine,
        in_specs=(rows, rows, rows, rows, columns, columns, units),
        out_specs=(rows, rows, columns, columns, units),
        check_vma=False,
    )
```

```python
import jax
import jax.numpy as jnp
from jax import lax
from jax.experimental import pallas as pl
from jax.experimental.pallas import tpu as pltpu
from jax.sharding import Mesh, PartitionSpec as P

NX_HI, NCORE, NY, NX_LO, NZ, RING, PLANE = 2, 2, 4, 2, 8, 4, 32
AXES = ("x_hi", "core", "y", "x_lo", "z")
EP, TP = ("x_hi", "core"), ("y", "x_lo", "z")
D, PAD, UNITS = 3072, 128, 128
F32, BF16 = jnp.float32, jnp.bfloat16
VMEM = pl.BlockSpec(memory_space=pltpu.VMEM)
SMEM = pl.BlockSpec(memory_space=pltpu.SMEM)
ORDER = (2, 1, 3)


def grant(mebibytes):
    return pltpu.CompilerParams(vmem_limit_bytes=mebibytes << 20)


def flat(x, core, y, z):
    return (((x // 2) * NCORE + core) * NY + y) * NX_LO * NZ + (x % 2) * NZ + z


def pairs(stage, d):
    out = []
    for x in range(RING):
        for core in range(NCORE):
            for y in range(RING):
                along_x = (stage == "light") == (core == 0)
                tx, ty = ((x + d) % RING, y) if along_x else (x, (y + d) % RING)
                out += [(flat(x, core, y, z), flat(tx, core, ty, z)) for z in range(NZ)]
    return out


def give(value, stage, d):
    return lax.ppermute(value, AXES, pairs(stage, d))


def fetch(value, stage, d):
    return lax.ppermute(value, AXES, pairs(stage, -d))


def swapped(value):
    return lax.ppermute(value, "core", [(0, 1), (1, 0)])


def exchanged(value, axis):
    return lax.all_to_all(value, axis, 0, 0, tiled=True)


def planes():
    along_x = [[flat(x, 0, y, z) for x in range(RING) for z in range(NZ)] for y in range(RING)]
    along_y = [[flat(x, 1, y, z) for y in range(RING) for z in range(NZ)] for x in range(RING)]
    return along_x + along_y


def scattered(value):
    return lax.all_to_all(value, AXES, 0, 0, axis_index_groups=planes(), tiled=True)


def dot(left, right, left_dim, right_dim):
    return lax.dot_general(
        left, right, (((left_dim,), (right_dim,)), ((), ())), preferred_element_type=F32
    )


def row_kernel(tokens, cotangent, routes, weights, out):
    lane = lax.broadcasted_iota(jnp.int32, (1, PAD), 1)
    r, w = routes[...], weights[...].astype(F32)
    gates = jnp.where(r[:, :1] == lane, w[:, :1], 0.0) + jnp.where(r[:, 1:] == lane, w[:, 1:], 0.0)
    first = jnp.concatenate([tokens[...].astype(F32), gates], axis=1)
    second = jnp.concatenate([cotangent[...].astype(F32), jnp.zeros((1, PAD), F32)], axis=1)
    both = jnp.concatenate([first, second], axis=0).astype(BF16)
    for i in range(NZ):
        out[i] = both


def copies_of_row(tokens, cotangent, routes, gate_weights):
    return pl.pallas_call(
        row_kernel,
        out_shape=jax.ShapeDtypeStruct((NZ, 2, D + PAD), BF16),
        out_specs=VMEM,
        name="copies_of_row",
    )(tokens, cotangent, routes, gate_weights)


def expert_kernel(group, rows, gate_slice, up_slice, down_slice, terms, acts):
    lane = lax.broadcasted_iota(jnp.int32, (rows.shape[0], PAD), 1)
    gates = jnp.where(lane == group[0], rows[:, 2 * D :].astype(F32), 0.0)
    column = jnp.sum(gates, axis=1, keepdims=True)
    x, cot = rows[:, :D], rows[:, D : 2 * D]
    gate_pre = dot(x, gate_slice[...], 1, 0)
    up_pre = dot(x, up_slice[...], 1, 0)
    grad_act = dot(cot, down_slice[...], 1, 1) * column
    sigmoid = jax.nn.sigmoid(gate_pre)
    silu = gate_pre * sigmoid
    hidden = (silu * up_pre * column).astype(BF16)
    grad_gpre = (grad_act * up_pre * (sigmoid * (1.0 + gate_pre * (1.0 - sigmoid)))).astype(BF16)
    grad_upre = (grad_act * silu).astype(BF16)
    acts[:, :UNITS] = hidden
    acts[:, UNITS : 2 * UNITS] = grad_gpre
    acts[:, 2 * UNITS :] = grad_upre
    terms[:, :D] = dot(hidden, down_slice[...], 1, 0).astype(terms.dtype)
    grad_rows = dot(grad_gpre, gate_slice[...], 1, 1) + dot(grad_upre, up_slice[...], 1, 1)
    terms[:, D:] = grad_rows.astype(terms.dtype)


def expert_terms(group, rows, gate_slice, up_slice, down_slice, kind):
    n = rows.shape[0]
    return pl.pallas_call(
        expert_kernel,
        out_shape=(
            jax.ShapeDtypeStruct((n, 2 * D), kind),
            jax.ShapeDtypeStruct((n, 3 * UNITS), BF16),
        ),
        in_specs=[SMEM] + [VMEM] * 4,
        out_specs=(VMEM, VMEM),
        compiler_params=grant(16),
        cost_estimate=pl.CostEstimate(
            flops=12 * n * D * UNITS, transcendentals=n * UNITS, bytes_accessed=4 * n * D + 6 * D * UNITS
        ),
        name="expert_terms",
    )(group, rows, gate_slice, up_slice, down_slice)


def weight_kernel(far, near, acts_far, acts_near, grad_g, grad_u, grad_d):
    u = UNITS

    def both(left_at, left_rows, right_at):
        def part(rows, acts):
            left = rows[:, left_at : left_at + D] if left_rows else acts[:, :u]
            right = acts[:, right_at : right_at + u] if left_rows else rows[:, D : 2 * D]
            return dot(left, right, 0, 0)

        return (part(far, acts_far) + part(near, acts_near)).astype(BF16)

    grad_g[0] = both(0, True, u)
    grad_u[0] = both(0, True, 2 * u)
    grad_d[0] = both(0, False, 0)


def weight_grads(far, near, acts_far, acts_near):
    n = 2 * far.shape[0]
    return pl.pallas_call(
        weight_kernel,
        out_shape=(
            jax.ShapeDtypeStruct((1, D, UNITS), BF16),
            jax.ShapeDtypeStruct((1, D, UNITS), BF16),
            jax.ShapeDtypeStruct((1, UNITS, D), BF16),
        ),
        in_specs=[VMEM] * 4,
        out_specs=(VMEM,) * 3,
        compiler_params=grant(8),
        cost_estimate=pl.CostEstimate(
            flops=6 * n * D * UNITS, transcendentals=0, bytes_accessed=4 * n * D + 6 * D * UNITS
        ),
        name="weight_grads",
    )(far, near, acts_far, acts_near)


def last_kernel(own, one, two, three, out):
    x, y = lax.axis_index(("x_hi", "x_lo")), lax.axis_index("y")
    place = jnp.where(lax.axis_index("core") == 0, x, y).astype(jnp.int32)
    for k, d in enumerate((0,) + ORDER):
        at = slice(k * NZ, (k + 1) * NZ)
        total = own[at] + one[at].astype(F32) + two[at].astype(F32) + three[at].astype(F32)
        first = lax.rem(place + d, RING) * NZ
        for i in range(NZ):
            row = total[i : i + 1]
            out[first + i] = jnp.concatenate([row[:, :D], row[:, D:]], axis=0).astype(BF16)


def summed_pairs(own, parts):
    return pl.pallas_call(
        last_kernel,
        out_shape=jax.ShapeDtypeStruct((PLANE, 2, D), BF16),
        in_specs=[VMEM] * 4,
        out_specs=VMEM,
        compiler_params=grant(2),
        name="summed_pairs",
    )(own, *parts)


def on_device(tokens, cotangent, routes, gate_weights, w_gate, w_up, w_down):
    slices = (w_gate[0], w_up[0], w_down[0])
    group = lax.axis_index(EP).astype(jnp.int32).reshape(1)
    with jax.named_scope("gather_z"):
        rows = exchanged(copies_of_row(tokens, cotangent, routes, gate_weights), "z")
        rows = jnp.concatenate([rows[:, 0, :D], rows[:, 1, :D], rows[:, 0, D:]], axis=1)
    with jax.named_scope("gather_light"):
        rows = jnp.concatenate([rows] + [fetch(rows, "light", d) for d in ORDER], axis=0)
    with jax.named_scope("gather_heavy"):
        near = [rows] + [fetch(rows, "heavy", d) for d in ORDER]
    with jax.named_scope("gather_core"):
        far = jnp.concatenate([swapped(chunk) for chunk in near], axis=0)
        near = jnp.concatenate(near, axis=0)
    with jax.named_scope("experts"):
        far_terms, far_acts = expert_terms(group, far, *slices, BF16)
        other = swapped(far_terms)
        near_terms, near_acts = expert_terms(group, near, *slices, F32)
    with jax.named_scope("weights"):
        grad_g, grad_u, grad_d = weight_grads(far, near, far_acts, near_acts)
    with jax.named_scope("reduce_heavy"):
        total = (near_terms + other.astype(F32)).reshape(RING, PLANE, 2 * D)
        got = [give(total[1 + i].astype(BF16), "heavy", d) for i, d in enumerate(ORDER)]
        *got, grad_g, grad_u, grad_d = lax.optimization_barrier((*got, grad_g, grad_u, grad_d))
    with jax.named_scope("reduce_plane"):
        got = scattered(summed_pairs(total[0], got))
        total = sum(got[i].astype(F32) for i in range(PLANE)).astype(BF16)
    return total[:1], total[1:], grad_g, grad_u, grad_d


def solution(mesh):
    fine = Mesh(mesh.devices.reshape(NX_HI, NCORE, NY, NX_LO, NZ), AXES)
    rows, columns, units = P(EP + TP, None), P(EP, None, TP), P(EP, TP, None)
    return jax.shard_map(
        on_device,
        mesh=fine,
        in_specs=(rows, rows, rows, rows, columns, columns, units),
        out_specs=(rows, rows, columns, columns, units),
        check_vma=False,
    )
```

```python
import jax
import jax.numpy as jnp
from jax import lax
from jax.experimental import pallas as pl
from jax.experimental.pallas import tpu as pltpu
from jax.sharding import Mesh, PartitionSpec as P

NX_HI, NCORE, NY, NX_LO, NZ, RING, PLANE = 2, 2, 4, 2, 8, 4, 32
AXES = ("x_hi", "core", "y", "x_lo", "z")
EP, TP = ("x_hi", "core"), ("y", "x_lo", "z")
D, PAD, UNITS = 3072, 128, 128
F32, BF16 = jnp.float32, jnp.bfloat16
VMEM = pl.BlockSpec(memory_space=pltpu.VMEM)
SMEM = pl.BlockSpec(memory_space=pltpu.SMEM)
ORDER, ISSUE = (2, 1, 3), (3, 1, 2)


def grant(mebibytes):
    return pltpu.CompilerParams(vmem_limit_bytes=mebibytes << 20)


def flat(x, core, y, z):
    return (((x // 2) * NCORE + core) * NY + y) * NX_LO * NZ + (x % 2) * NZ + z


def pairs(stage, d):
    out = []
    for x in range(RING):
        for core in range(NCORE):
            for y in range(RING):
                along_x = (stage == "light") == (core == 0)
                tx, ty = ((x + d) % RING, y) if along_x else (x, (y + d) % RING)
                out += [(flat(x, core, y, z), flat(tx, core, ty, z)) for z in range(NZ)]
    return out


def give(value, stage, d):
    return lax.ppermute(value, AXES, pairs(stage, d))


def fetch(value, stage, d):
    return lax.ppermute(value, AXES, pairs(stage, -d))


def swapped(value):
    return lax.ppermute(value, "core", [(0, 1), (1, 0)])


def exchanged(value, axis):
    return lax.all_to_all(value, axis, 0, 0, tiled=True)


def planes():
    along_x = [[flat(x, 0, y, z) for x in range(RING) for z in range(NZ)] for y in range(RING)]
    along_y = [[flat(x, 1, y, z) for y in range(RING) for z in range(NZ)] for x in range(RING)]
    return along_x + along_y


def scattered(value):
    return lax.all_to_all(value, AXES, 0, 0, axis_index_groups=planes(), tiled=True)


def dot(left, right, left_dim, right_dim):
    return lax.dot_general(
        left, right, (((left_dim,), (right_dim,)), ((), ())), preferred_element_type=F32
    )


def row_kernel(tokens, cotangent, routes, weights, out):
    lane = lax.broadcasted_iota(jnp.int32, (1, PAD), 1)
    r, w = routes[...], weights[...].astype(F32)
    gates = jnp.where(r[:, :1] == lane, w[:, :1], 0.0) + jnp.where(r[:, 1:] == lane, w[:, 1:], 0.0)
    first = jnp.concatenate([tokens[...].astype(F32), gates], axis=1)
    second = jnp.concatenate([cotangent[...].astype(F32), jnp.zeros((1, PAD), F32)], axis=1)
    both = jnp.concatenate([first, second], axis=0).astype(BF16)
    for i in range(NZ):
        out[i] = both


def copies_of_row(tokens, cotangent, routes, gate_weights):
    return pl.pallas_call(
        row_kernel,
        out_shape=jax.ShapeDtypeStruct((NZ, 2, D + PAD), BF16),
        out_specs=VMEM,
        name="copies_of_row",
    )(tokens, cotangent, routes, gate_weights)


def expert_kernel(group, rows, gate_slice, up_slice, down_slice, terms, acts):
    lane = lax.broadcasted_iota(jnp.int32, (rows.shape[0], PAD), 1)
    gates = jnp.where(lane == group[0], rows[:, 2 * D :].astype(F32), 0.0)
    column = jnp.sum(gates, axis=1, keepdims=True)
    x, cot = rows[:, :D], rows[:, D : 2 * D]
    gate_pre = dot(x, gate_slice[...], 1, 0)
    up_pre = dot(x, up_slice[...], 1, 0)
    grad_act = dot(cot, down_slice[...], 1, 1) * column
    sigmoid = jax.nn.sigmoid(gate_pre)
    silu = gate_pre * sigmoid
    hidden = (silu * up_pre * column).astype(BF16)
    grad_gpre = (grad_act * up_pre * (sigmoid * (1.0 + gate_pre * (1.0 - sigmoid)))).astype(BF16)
    grad_upre = (grad_act * silu).astype(BF16)
    acts[:, :UNITS] = hidden
    acts[:, UNITS : 2 * UNITS] = grad_gpre
    acts[:, 2 * UNITS :] = grad_upre
    terms[:, :D] = dot(hidden, down_slice[...], 1, 0).astype(terms.dtype)
    grad_rows = dot(grad_gpre, gate_slice[...], 1, 1) + dot(grad_upre, up_slice[...], 1, 1)
    terms[:, D:] = grad_rows.astype(terms.dtype)


def expert_terms(group, rows, gate_slice, up_slice, down_slice, kind):
    n = rows.shape[0]
    return pl.pallas_call(
        expert_kernel,
        out_shape=(
            jax.ShapeDtypeStruct((n, 2 * D), kind),
            jax.ShapeDtypeStruct((n, 3 * UNITS), BF16),
        ),
        in_specs=[SMEM] + [VMEM] * 4,
        out_specs=(VMEM, VMEM),
        compiler_params=grant(16),
        cost_estimate=pl.CostEstimate(
            flops=12 * n * D * UNITS, transcendentals=n * UNITS, bytes_accessed=4 * n * D + 6 * D * UNITS
        ),
        name="expert_terms",
    )(group, rows, gate_slice, up_slice, down_slice)


def weight_kernel(*refs):
    u, parts = UNITS, len(refs) // 2
    grad_g, grad_u, grad_d = refs[-3:]
    pairs_of = list(zip(refs[: parts - 1], refs[parts - 1 : -3]))
    for grad, at in ((grad_g, u), (grad_u, 2 * u)):
        total = sum(dot(rows[:, :D], acts[:, at : at + u], 0, 0) for rows, acts in pairs_of)
        grad[0] = total.astype(BF16)
    total = sum(dot(acts[:, :u], rows[:, D : 2 * D], 0, 0) for rows, acts in pairs_of)
    grad_d[0] = total.astype(BF16)


def weight_grads(rows, acts):
    n = sum(r.shape[0] for r in rows)
    return pl.pallas_call(
        weight_kernel,
        out_shape=(
            jax.ShapeDtypeStruct((1, D, UNITS), BF16),
            jax.ShapeDtypeStruct((1, D, UNITS), BF16),
            jax.ShapeDtypeStruct((1, UNITS, D), BF16),
        ),
        in_specs=[VMEM] * (len(rows) + len(acts)),
        out_specs=(VMEM,) * 3,
        compiler_params=grant(8),
        cost_estimate=pl.CostEstimate(
            flops=6 * n * D * UNITS, transcendentals=0, bytes_accessed=4 * n * D + 6 * D * UNITS
        ),
        name="weight_grads",
    )(*rows, *acts)


def last_kernel(own, one, two, three, out):
    x, y = lax.axis_index(("x_hi", "x_lo")), lax.axis_index("y")
    place = jnp.where(lax.axis_index("core") == 0, x, y).astype(jnp.int32)
    for k, d in enumerate((0,) + ORDER):
        at = slice(k * NZ, (k + 1) * NZ)
        total = own[at] + one[at].astype(F32) + two[at].astype(F32) + three[at].astype(F32)
        first = lax.rem(place + d, RING) * NZ
        for i in range(NZ):
            row = total[i : i + 1]
            out[first + i] = jnp.concatenate([row[:, :D], row[:, D:]], axis=0).astype(BF16)


def summed_pairs(own, parts):
    return pl.pallas_call(
        last_kernel,
        out_shape=jax.ShapeDtypeStruct((PLANE, 2, D), BF16),
        in_specs=[VMEM] * 4,
        out_specs=VMEM,
        compiler_params=grant(2),
        name="summed_pairs",
    )(own, *parts)


def on_device(tokens, cotangent, routes, gate_weights, w_gate, w_up, w_down):
    slices = (w_gate[0], w_up[0], w_down[0])
    group = lax.axis_index(EP).astype(jnp.int32).reshape(1)
    with jax.named_scope("gather_z"):
        rows = exchanged(copies_of_row(tokens, cotangent, routes, gate_weights), "z")
        rows = jnp.concatenate([rows[:, 0, :D], rows[:, 1, :D], rows[:, 0, D:]], axis=1)
    with jax.named_scope("gather_light"):
        got = {d: fetch(rows, "light", d) for d in (2, 3, 1)}
        rows = jnp.concatenate([rows] + [got[d] for d in ORDER], axis=0)
    with jax.named_scope("gather_heavy"):
        got = {d: fetch(rows, "heavy", d) for d in ISSUE}
    with jax.named_scope("gather_core"):
        own, got[2] = lax.optimization_barrier((rows, got[2]))
        far = {d: swapped(got[d]) for d in ORDER}
        far_one = jnp.concatenate([swapped(own), far[2]], axis=0)
        far_two = jnp.concatenate([far[1], far[3]], axis=0)
        near = jnp.concatenate([own] + [got[d] for d in ORDER], axis=0)
    with jax.named_scope("experts"):
        terms_one, acts_one = expert_terms(group, far_one, *slices, BF16)
        other_one = swapped(terms_one)
        terms_two, acts_two = expert_terms(group, far_two, *slices, BF16)
        other_two = swapped(terms_two)
        near_terms, near_acts = expert_terms(group, near, *slices, F32)
    with jax.named_scope("weights"):
        grads = weight_grads((far_one, far_two, near), (acts_one, acts_two, near_acts))
    with jax.named_scope("reduce_heavy"):
        half = 2 * PLANE
        one = near_terms[:half] + other_one.astype(F32)
        two = near_terms[half:] + other_two.astype(F32)
        send = {1: two[:PLANE], 2: one[PLANE:], 3: two[PLANE:]}
        got = {d: give(send[d].astype(BF16), "heavy", d) for d in ISSUE}
        got = [got[d] for d in ORDER]
        *got, grad_g, grad_u, grad_d = lax.optimization_barrier((*got, *grads))
    with jax.named_scope("reduce_plane"):
        got = scattered(summed_pairs(one[:PLANE], got))
        total = sum(got[i].astype(F32) for i in range(PLANE)).astype(BF16)
    return total[:1], total[1:], grad_g, grad_u, grad_d


def solution(mesh):
    fine = Mesh(mesh.devices.reshape(NX_HI, NCORE, NY, NX_LO, NZ), AXES)
    rows, columns, units = P(EP + TP, None), P(EP, None, TP), P(EP, TP, None)
    return jax.shard_map(
        on_device,
        mesh=fine,
        in_specs=(rows, rows, rows, rows, columns, columns, units),
        out_specs=(rows, rows, columns, columns, units),
        check_vma=False,
    )
```

```python
import jax
import jax.numpy as jnp
from jax import lax
from jax.experimental import pallas as pl
from jax.experimental.pallas import tpu as pltpu
from jax.sharding import Mesh, PartitionSpec as P

NX_HI, NCORE, NY, NX_LO, NZ, RING, PLANE = 2, 2, 4, 2, 8, 4, 32
AXES = ("x_hi", "core", "y", "x_lo", "z")
EP, TP = ("x_hi", "core"), ("y", "x_lo", "z")
D, PAD, UNITS = 3072, 128, 128
F32, BF16 = jnp.float32, jnp.bfloat16
VMEM = pl.BlockSpec(memory_space=pltpu.VMEM)
SMEM = pl.BlockSpec(memory_space=pltpu.SMEM)
ORDER, ISSUE = (2, 1, 3), (3, 1, 2)


def grant(mebibytes):
    return pltpu.CompilerParams(vmem_limit_bytes=mebibytes << 20)


def flat(x, core, y, z):
    return (((x // 2) * NCORE + core) * NY + y) * NX_LO * NZ + (x % 2) * NZ + z


def pairs(stage, d):
    out = []
    for x in range(RING):
        for core in range(NCORE):
            for y in range(RING):
                along_x = (stage == "light") == (core == 0)
                tx, ty = ((x + d) % RING, y) if along_x else (x, (y + d) % RING)
                out += [(flat(x, core, y, z), flat(tx, core, ty, z)) for z in range(NZ)]
    return out


def give(value, stage, d):
    return lax.ppermute(value, AXES, pairs(stage, d))


def fetch(value, stage, d):
    return lax.ppermute(value, AXES, pairs(stage, -d))


def swapped(value):
    return lax.ppermute(value, "core", [(0, 1), (1, 0)])


def exchanged(value, axis):
    return lax.all_to_all(value, axis, 0, 0, tiled=True)


def planes():
    along_x = [[flat(x, 0, y, z) for x in range(RING) for z in range(NZ)] for y in range(RING)]
    along_y = [[flat(x, 1, y, z) for y in range(RING) for z in range(NZ)] for x in range(RING)]
    return along_x + along_y


def scattered(value):
    return lax.all_to_all(value, AXES, 0, 0, axis_index_groups=planes(), tiled=True)


def dot(left, right, left_dim, right_dim):
    return lax.dot_general(
        left, right, (((left_dim,), (right_dim,)), ((), ())), preferred_element_type=F32
    )


def row_kernel(tokens, cotangent, routes, weights, out):
    lane = lax.broadcasted_iota(jnp.int32, (1, PAD), 1)
    r, w = routes[...], weights[...].astype(F32)
    gates = jnp.where(r[:, :1] == lane, w[:, :1], 0.0) + jnp.where(r[:, 1:] == lane, w[:, 1:], 0.0)
    first = jnp.concatenate([tokens[...].astype(F32), gates], axis=1)
    second = jnp.concatenate([cotangent[...].astype(F32), jnp.zeros((1, PAD), F32)], axis=1)
    both = jnp.concatenate([first, second], axis=0).astype(BF16)
    for i in range(NZ):
        out[i] = both


def copies_of_row(tokens, cotangent, routes, gate_weights):
    return pl.pallas_call(
        row_kernel,
        out_shape=jax.ShapeDtypeStruct((NZ, 2, D + PAD), BF16),
        out_specs=VMEM,
        name="copies_of_row",
    )(tokens, cotangent, routes, gate_weights)


def expert_kernel(group, rows, pair_slice, down_slice, terms, acts):
    lane = lax.broadcasted_iota(jnp.int32, (rows.shape[0], PAD), 1)
    gates = jnp.where(lane == group[0], rows[:, 2 * D :].astype(F32), 0.0)
    column = jnp.sum(gates, axis=1, keepdims=True)
    x, cot = rows[:, :D], rows[:, D : 2 * D]
    pre = dot(x, pair_slice[...], 1, 0)
    gate_pre, up_pre = pre[:, :UNITS], pre[:, UNITS:]
    grad_act = dot(cot, down_slice[...], 1, 1) * column
    sigmoid = jax.nn.sigmoid(gate_pre)
    silu = gate_pre * sigmoid
    hidden = (silu * up_pre * column).astype(BF16)
    grad_gpre = (grad_act * up_pre * (sigmoid * (1.0 + gate_pre * (1.0 - sigmoid)))).astype(BF16)
    grad_upre = (grad_act * silu).astype(BF16)
    acts[:, :UNITS] = hidden
    acts[:, UNITS : 2 * UNITS] = grad_gpre
    acts[:, 2 * UNITS :] = grad_upre
    terms[:, :D] = dot(hidden, down_slice[...], 1, 0).astype(terms.dtype)
    grad_rows = dot(acts[:, UNITS:], pair_slice[...], 1, 1)
    terms[:, D:] = grad_rows.astype(terms.dtype)


def expert_terms(group, rows, pair_slice, down_slice, kind):
    n = rows.shape[0]
    return pl.pallas_call(
        expert_kernel,
        out_shape=(
            jax.ShapeDtypeStruct((n, 2 * D), kind),
            jax.ShapeDtypeStruct((n, 3 * UNITS), BF16),
        ),
        in_specs=[SMEM] + [VMEM] * 3,
        out_specs=(VMEM, VMEM),
        compiler_params=grant(16),
        cost_estimate=pl.CostEstimate(
            flops=12 * n * D * UNITS, transcendentals=n * UNITS, bytes_accessed=4 * n * D + 6 * D * UNITS
        ),
        name="expert_terms",
    )(group, rows, pair_slice, down_slice)


def weight_kernel(*refs):
    u, parts = UNITS, len(refs) // 2
    grad_g, grad_u, grad_d = refs[-3:]
    pairs_of = list(zip(refs[: parts - 1], refs[parts - 1 : -3]))
    for grad, at in ((grad_g, u), (grad_u, 2 * u)):
        total = sum(dot(rows[:, :D], acts[:, at : at + u], 0, 0) for rows, acts in pairs_of)
        grad[0] = total.astype(BF16)
    total = sum(dot(acts[:, :u], rows[:, D : 2 * D], 0, 0) for rows, acts in pairs_of)
    grad_d[0] = total.astype(BF16)


def weight_grads(rows, acts):
    n = sum(r.shape[0] for r in rows)
    return pl.pallas_call(
        weight_kernel,
        out_shape=(
            jax.ShapeDtypeStruct((1, D, UNITS), BF16),
            jax.ShapeDtypeStruct((1, D, UNITS), BF16),
            jax.ShapeDtypeStruct((1, UNITS, D), BF16),
        ),
        in_specs=[VMEM] * (len(rows) + len(acts)),
        out_specs=(VMEM,) * 3,
        compiler_params=grant(8),
        cost_estimate=pl.CostEstimate(
            flops=6 * n * D * UNITS, transcendentals=0, bytes_accessed=4 * n * D + 6 * D * UNITS
        ),
        name="weight_grads",
    )(*rows, *acts)


def last_kernel(own, one, two, three, out):
    x, y = lax.axis_index(("x_hi", "x_lo")), lax.axis_index("y")
    place = jnp.where(lax.axis_index("core") == 0, x, y).astype(jnp.int32)
    for k, d in enumerate((0,) + ORDER):
        at = slice(k * NZ, (k + 1) * NZ)
        total = own[at] + one[at].astype(F32) + two[at].astype(F32) + three[at].astype(F32)
        first = lax.rem(place + d, RING) * NZ
        for i in range(NZ):
            row = total[i : i + 1]
            out[first + i] = jnp.concatenate([row[:, :D], row[:, D:]], axis=0).astype(BF16)


def summed_pairs(own, parts):
    return pl.pallas_call(
        last_kernel,
        out_shape=jax.ShapeDtypeStruct((PLANE, 2, D), BF16),
        in_specs=[VMEM] * 4,
        out_specs=VMEM,
        compiler_params=grant(2),
        name="summed_pairs",
    )(own, *parts)


def on_device(tokens, cotangent, routes, gate_weights, w_gate, w_up, w_down):
    group = lax.axis_index(EP).astype(jnp.int32).reshape(1)
    with jax.named_scope("gather_z"):
        rows = exchanged(copies_of_row(tokens, cotangent, routes, gate_weights), "z")
        rows = jnp.concatenate([rows[:, 0, :D], rows[:, 1, :D], rows[:, 0, D:]], axis=1)
    with jax.named_scope("gather_light"):
        got = {d: fetch(rows, "light", d) for d in ISSUE}
        first = lax.optimization_barrier(jnp.concatenate([rows, got[2]], axis=0))
        rows = jnp.concatenate([first, got[1], got[3]], axis=0)
    with jax.named_scope("gather_heavy"):
        got = {d: fetch(rows, "heavy", d) for d in ISSUE}
    with jax.named_scope("gather_core"):
        own, got[2], gate_slice = lax.optimization_barrier((rows, got[2], w_gate[0]))
        slices = (jnp.concatenate([gate_slice, w_up[0]], axis=1), w_down[0])
        far = {d: swapped(got[d]) for d in ORDER}
        far_one = jnp.concatenate([swapped(own), far[2]], axis=0)
        far_two = jnp.concatenate([far[1], far[3]], axis=0)
        near = jnp.concatenate([own] + [got[d] for d in ORDER], axis=0)
    with jax.named_scope("experts"):
        terms_one, acts_one = expert_terms(group, far_one, *slices, BF16)
        other_one = swapped(terms_one)
        _, far_two = lax.optimization_barrier((terms_one, far_two))
        terms_two, acts_two = expert_terms(group, far_two, *slices, BF16)
        other_two = swapped(terms_two)
        near_terms, near_acts = expert_terms(group, near, *slices, F32)
    with jax.named_scope("weights"):
        grads = weight_grads((far_one, far_two, near), (acts_one, acts_two, near_acts))
    with jax.named_scope("reduce_heavy"):
        half = 2 * PLANE
        one = near_terms[:half] + other_one.astype(F32)
        two = near_terms[half:] + other_two.astype(F32)
        send = {1: two[:PLANE], 2: one[PLANE:], 3: two[PLANE:]}
        got = {d: give(send[d].astype(BF16), "heavy", d) for d in ISSUE}
        got = [got[d] for d in ORDER]
        *got, grad_g, grad_u, grad_d = lax.optimization_barrier((*got, *grads))
    with jax.named_scope("reduce_plane"):
        got = scattered(summed_pairs(one[:PLANE], got))
        total = sum(got[i].astype(F32) for i in range(PLANE)).astype(BF16)
    return total[:1], total[1:], grad_g, grad_u, grad_d


def solution(mesh):
    fine = Mesh(mesh.devices.reshape(NX_HI, NCORE, NY, NX_LO, NZ), AXES)
    rows, columns, units = P(EP + TP, None), P(EP, None, TP), P(EP, TP, None)
    return jax.shard_map(
        on_device,
        mesh=fine,
        in_specs=(rows, rows, rows, rows, columns, columns, units),
        out_specs=(rows, rows, columns, columns, units),
        check_vma=False,
    )
```

```python
import jax
import jax.numpy as jnp
from jax import lax
from jax.experimental import pallas as pl
from jax.experimental.pallas import tpu as pltpu
from jax.sharding import Mesh, PartitionSpec as P

NX_HI, NCORE, NY, NX_LO, NZ, RING, PLANE = 2, 2, 4, 2, 8, 4, 32
AXES = ("x_hi", "core", "y", "x_lo", "z")
EP, TP = ("x_hi", "core"), ("y", "x_lo", "z")
D, PAD, UNITS = 3072, 128, 128
F32, BF16 = jnp.float32, jnp.bfloat16
VMEM = pl.BlockSpec(memory_space=pltpu.VMEM)
SMEM = pl.BlockSpec(memory_space=pltpu.SMEM)
ORDER, ISSUE = (2, 1, 3), (3, 1, 2)


def grant(mebibytes):
    return pltpu.CompilerParams(vmem_limit_bytes=mebibytes << 20)


def flat(x, core, y, z):
    return (((x // 2) * NCORE + core) * NY + y) * NX_LO * NZ + (x % 2) * NZ + z


def pairs(stage, d):
    out = []
    for x in range(RING):
        for core in range(NCORE):
            for y in range(RING):
                along_x = (stage == "light") == (core == 0)
                tx, ty = ((x + d) % RING, y) if along_x else (x, (y + d) % RING)
                out += [(flat(x, core, y, z), flat(tx, core, ty, z)) for z in range(NZ)]
    return out


def give(value, stage, d):
    return lax.ppermute(value, AXES, pairs(stage, d))


def fetch(value, stage, d):
    return lax.ppermute(value, AXES, pairs(stage, -d))


def swapped(value):
    return lax.ppermute(value, "core", [(0, 1), (1, 0)])


def exchanged(value, axis):
    return lax.all_to_all(value, axis, 0, 0, tiled=True)


def planes():
    along_x = [[flat(x, 0, y, z) for x in range(RING) for z in range(NZ)] for y in range(RING)]
    along_y = [[flat(x, 1, y, z) for y in range(RING) for z in range(NZ)] for x in range(RING)]
    return along_x + along_y


def scattered(value):
    return lax.all_to_all(value, AXES, 0, 0, axis_index_groups=planes(), tiled=True)


def dot(left, right, left_dim, right_dim):
    return lax.dot_general(
        left, right, (((left_dim,), (right_dim,)), ((), ())), preferred_element_type=F32
    )


def row_kernel(tokens, cotangent, routes, weights, out):
    lane = lax.broadcasted_iota(jnp.int32, (1, PAD), 1)
    r, w = routes[...], weights[...].astype(F32)
    gates = jnp.where(r[:, :1] == lane, w[:, :1], 0.0) + jnp.where(r[:, 1:] == lane, w[:, 1:], 0.0)
    first = jnp.concatenate([tokens[...].astype(F32), gates], axis=1)
    second = jnp.concatenate([cotangent[...].astype(F32), jnp.zeros((1, PAD), F32)], axis=1)
    both = jnp.concatenate([first, second], axis=0).astype(BF16)
    for i in range(NZ):
        out[i] = both


def copies_of_row(tokens, cotangent, routes, gate_weights):
    return pl.pallas_call(
        row_kernel,
        out_shape=jax.ShapeDtypeStruct((NZ, 2, D + PAD), BF16),
        out_specs=VMEM,
        name="copies_of_row",
    )(tokens, cotangent, routes, gate_weights)


def expert_kernel(group, rows, pair_slice, down_slice, terms, acts):
    lane = lax.broadcasted_iota(jnp.int32, (rows.shape[0], PAD), 1)
    gates = jnp.where(lane == group[0], rows[:, 2 * D :].astype(F32), 0.0)
    column = jnp.sum(gates, axis=1, keepdims=True)
    x, cot = rows[:, :D], rows[:, D : 2 * D]
    pre = dot(x, pair_slice[...], 1, 0)
    gate_pre, up_pre = pre[:, :UNITS], pre[:, UNITS:]
    grad_act = dot(cot, down_slice[...], 1, 1) * column
    sigmoid = jax.nn.sigmoid(gate_pre)
    silu = gate_pre * sigmoid
    hidden = (silu * up_pre * column).astype(BF16)
    grad_gpre = (grad_act * up_pre * (sigmoid * (1.0 + gate_pre * (1.0 - sigmoid)))).astype(BF16)
    grad_upre = (grad_act * silu).astype(BF16)
    acts[:, :UNITS] = hidden
    acts[:, UNITS : 2 * UNITS] = grad_gpre
    acts[:, 2 * UNITS :] = grad_upre
    terms[:, :D] = dot(hidden, down_slice[...], 1, 0).astype(terms.dtype)
    grad_rows = dot(acts[:, UNITS:], pair_slice[...], 1, 1)
    terms[:, D:] = grad_rows.astype(terms.dtype)


def expert_terms(group, rows, pair_slice, down_slice, kind):
    n = rows.shape[0]
    return pl.pallas_call(
        expert_kernel,
        out_shape=(
            jax.ShapeDtypeStruct((n, 2 * D), kind),
            jax.ShapeDtypeStruct((n, 3 * UNITS), BF16),
        ),
        in_specs=[SMEM] + [VMEM] * 3,
        out_specs=(VMEM, VMEM),
        compiler_params=grant(16),
        cost_estimate=pl.CostEstimate(
            flops=12 * n * D * UNITS, transcendentals=n * UNITS, bytes_accessed=4 * n * D + 6 * D * UNITS
        ),
        name="expert_terms",
    )(group, rows, pair_slice, down_slice)


def weight_kernel(*refs):
    u, parts = UNITS, len(refs) // 2
    grad_g, grad_u, grad_d = refs[-3:]
    pairs_of = list(zip(refs[: parts - 1], refs[parts - 1 : -3]))
    for grad, at in ((grad_g, u), (grad_u, 2 * u)):
        total = sum(dot(rows[:, :D], acts[:, at : at + u], 0, 0) for rows, acts in pairs_of)
        grad[0] = total.astype(BF16)
    total = sum(dot(acts[:, :u], rows[:, D : 2 * D], 0, 0) for rows, acts in pairs_of)
    grad_d[0] = total.astype(BF16)


def weight_grads(rows, acts):
    n = sum(r.shape[0] for r in rows)
    return pl.pallas_call(
        weight_kernel,
        out_shape=(
            jax.ShapeDtypeStruct((1, D, UNITS), BF16),
            jax.ShapeDtypeStruct((1, D, UNITS), BF16),
            jax.ShapeDtypeStruct((1, UNITS, D), BF16),
        ),
        in_specs=[VMEM] * (len(rows) + len(acts)),
        out_specs=(VMEM,) * 3,
        compiler_params=grant(8),
        cost_estimate=pl.CostEstimate(
            flops=6 * n * D * UNITS, transcendentals=0, bytes_accessed=4 * n * D + 6 * D * UNITS
        ),
        name="weight_grads",
    )(*rows, *acts)


def last_kernel(own, one, two, three, out):
    x, y = lax.axis_index(("x_hi", "x_lo")), lax.axis_index("y")
    place = jnp.where(lax.axis_index("core") == 0, x, y).astype(jnp.int32)
    for k, d in enumerate((0,) + ORDER):
        at = slice(k * NZ, (k + 1) * NZ)
        total = own[at] + one[at].astype(F32) + two[at].astype(F32) + three[at].astype(F32)
        first = lax.rem(place + d, RING) * NZ
        for i in range(NZ):
            row = total[i : i + 1]
            out[first + i] = jnp.concatenate([row[:, :D], row[:, D:]], axis=0).astype(BF16)


def summed_pairs(own, parts):
    return pl.pallas_call(
        last_kernel,
        out_shape=jax.ShapeDtypeStruct((PLANE, 2, D), BF16),
        in_specs=[VMEM] * 4,
        out_specs=VMEM,
        compiler_params=grant(2),
        name="summed_pairs",
    )(own, *parts)


def on_device(tokens, cotangent, routes, gate_weights, w_gate, w_up, w_down):
    group = lax.axis_index(EP).astype(jnp.int32).reshape(1)
    with jax.named_scope("gather_z"):
        rows = exchanged(copies_of_row(tokens, cotangent, routes, gate_weights), "z")
        rows = jnp.concatenate([rows[:, 0, :D], rows[:, 1, :D], rows[:, 0, D:]], axis=1)
    with jax.named_scope("gather_light"):
        got = {d: fetch(rows, "light", d) for d in ISSUE}
        rows = jnp.concatenate([rows] + [got[d] for d in ORDER], axis=0)
    with jax.named_scope("gather_heavy"):
        got = {d: fetch(rows, "heavy", d) for d in ISSUE}
    with jax.named_scope("gather_core"):
        own, got[2], gate_slice = lax.optimization_barrier((rows, got[2], w_gate[0]))
        slices = (jnp.concatenate([gate_slice, w_up[0]], axis=1), w_down[0])
        near_one = jnp.concatenate([own, got[2]], axis=0)
        far_one = jnp.concatenate([swapped(own), swapped(got[2])], axis=0)
    with jax.named_scope("experts"):
        near_terms_one, near_acts_one = expert_terms(group, near_one, *slices, F32)
        near_terms_one, got[1], got[3] = lax.optimization_barrier((near_terms_one, got[1], got[3]))
        near_two = jnp.concatenate([got[1], got[3]], axis=0)
        far_two = jnp.concatenate([swapped(got[1]), swapped(got[3])], axis=0)
        terms_one, acts_one = expert_terms(group, far_one, *slices, BF16)
        other_one = swapped(terms_one)
        _, far_two = lax.optimization_barrier((terms_one, far_two))
        terms_two, acts_two = expert_terms(group, far_two, *slices, BF16)
        other_two = swapped(terms_two)
        _, near_two = lax.optimization_barrier((terms_two, near_two))
        near_terms_two, near_acts_two = expert_terms(group, near_two, *slices, F32)
    with jax.named_scope("weights"):
        rows = (far_one, far_two, near_one, near_two)
        grads = weight_grads(rows, (acts_one, acts_two, near_acts_one, near_acts_two))
    with jax.named_scope("reduce_heavy"):
        one = near_terms_one + other_one.astype(F32)
        two = near_terms_two + other_two.astype(F32)
        send = {1: two[:PLANE], 2: one[PLANE:], 3: two[PLANE:]}
        got = {d: give(send[d].astype(BF16), "heavy", d) for d in ISSUE}
        got = [got[d] for d in ORDER]
        *got, grad_g, grad_u, grad_d = lax.optimization_barrier((*got, *grads))
    with jax.named_scope("reduce_plane"):
        got = scattered(summed_pairs(one[:PLANE], got))
        total = sum(got[i].astype(F32) for i in range(PLANE)).astype(BF16)
    return total[:1], total[1:], grad_g, grad_u, grad_d


def solution(mesh):
    fine = Mesh(mesh.devices.reshape(NX_HI, NCORE, NY, NX_LO, NZ), AXES)
    rows, columns, units = P(EP + TP, None), P(EP, None, TP), P(EP, TP, None)
    return jax.shard_map(
        on_device,
        mesh=fine,
        in_specs=(rows, rows, rows, rows, columns, columns, units),
        out_specs=(rows, rows, columns, columns, units),
        check_vma=False,
    )
```

```python
import jax
import jax.numpy as jnp
from jax import lax
from jax.experimental import pallas as pl
from jax.experimental.pallas import tpu as pltpu
from jax.sharding import Mesh, PartitionSpec as P

NX_HI, NCORE, NY, NX_LO, NZ, RING, PLANE = 2, 2, 4, 2, 8, 4, 32
AXES = ("x_hi", "core", "y", "x_lo", "z")
EP, TP = ("x_hi", "core"), ("y", "x_lo", "z")
D, PAD, UNITS = 3072, 128, 128
F32, BF16 = jnp.float32, jnp.bfloat16
VMEM = pl.BlockSpec(memory_space=pltpu.VMEM)
SMEM = pl.BlockSpec(memory_space=pltpu.SMEM)
ORDER, ISSUE = (2, 1, 3), (3, 1, 2)


def grant(mebibytes):
    return pltpu.CompilerParams(vmem_limit_bytes=mebibytes << 20)


def flat(x, core, y, z):
    return (((x // 2) * NCORE + core) * NY + y) * NX_LO * NZ + (x % 2) * NZ + z


def pairs(stage, d):
    out = []
    for x in range(RING):
        for core in range(NCORE):
            for y in range(RING):
                along_x = (stage == "light") == (core == 0)
                tx, ty = ((x + d) % RING, y) if along_x else (x, (y + d) % RING)
                out += [(flat(x, core, y, z), flat(tx, core, ty, z)) for z in range(NZ)]
    return out


def give(value, stage, d):
    return lax.ppermute(value, AXES, pairs(stage, d))


def fetch(value, stage, d):
    return lax.ppermute(value, AXES, pairs(stage, -d))


def swapped(value):
    return lax.ppermute(value, "core", [(0, 1), (1, 0)])


def exchanged(value, axis):
    return lax.all_to_all(value, axis, 0, 0, tiled=True)


def planes():
    along_x = [[flat(x, 0, y, z) for x in range(RING) for z in range(NZ)] for y in range(RING)]
    along_y = [[flat(x, 1, y, z) for y in range(RING) for z in range(NZ)] for x in range(RING)]
    return along_x + along_y


def scattered(value):
    return lax.all_to_all(value, AXES, 0, 0, axis_index_groups=planes(), tiled=True)


def dot(left, right, left_dim, right_dim):
    return lax.dot_general(
        left, right, (((left_dim,), (right_dim,)), ((), ())), preferred_element_type=F32
    )


def row_kernel(tokens, cotangent, routes, weights, out):
    lane = lax.broadcasted_iota(jnp.int32, (1, PAD), 1)
    r, w = routes[...], weights[...].astype(F32)
    gates = jnp.where(r[:, :1] == lane, w[:, :1], 0.0) + jnp.where(r[:, 1:] == lane, w[:, 1:], 0.0)
    first = jnp.concatenate([tokens[...].astype(F32), gates], axis=1)
    second = jnp.concatenate([cotangent[...].astype(F32), jnp.zeros((1, PAD), F32)], axis=1)
    both = jnp.concatenate([first, second], axis=0).astype(BF16)
    for i in range(NZ):
        out[i] = both


def copies_of_row(tokens, cotangent, routes, gate_weights):
    return pl.pallas_call(
        row_kernel,
        out_shape=jax.ShapeDtypeStruct((NZ, 2, D + PAD), BF16),
        out_specs=VMEM,
        name="copies_of_row",
    )(tokens, cotangent, routes, gate_weights)


def expert_kernel(group, rows, pair_slice, down_slice, terms, acts):
    lane = lax.broadcasted_iota(jnp.int32, (rows.shape[0], PAD), 1)
    gates = jnp.where(lane == group[0], rows[:, 2 * D :].astype(F32), 0.0)
    column = jnp.sum(gates, axis=1, keepdims=True)
    x, cot = rows[:, :D], rows[:, D : 2 * D]
    pre = dot(x, pair_slice[...], 1, 0)
    gate_pre, up_pre = pre[:, :UNITS], pre[:, UNITS:]
    grad_act = dot(cot, down_slice[...], 1, 1) * column
    sigmoid = jax.nn.sigmoid(gate_pre)
    silu = gate_pre * sigmoid
    hidden = (silu * up_pre * column).astype(BF16)
    grad_gpre = (grad_act * up_pre * (sigmoid * (1.0 + gate_pre * (1.0 - sigmoid)))).astype(BF16)
    grad_upre = (grad_act * silu).astype(BF16)
    acts[:, :UNITS] = hidden
    acts[:, UNITS : 2 * UNITS] = grad_gpre
    acts[:, 2 * UNITS :] = grad_upre
    terms[:, :D] = dot(hidden, down_slice[...], 1, 0).astype(terms.dtype)
    grad_rows = dot(acts[:, UNITS:], pair_slice[...], 1, 1)
    terms[:, D:] = grad_rows.astype(terms.dtype)


def expert_terms(group, rows, pair_slice, down_slice, kind):
    n = rows.shape[0]
    return pl.pallas_call(
        expert_kernel,
        out_shape=(
            jax.ShapeDtypeStruct((n, 2 * D), kind),
            jax.ShapeDtypeStruct((n, 3 * UNITS), BF16),
        ),
        in_specs=[SMEM] + [VMEM] * 3,
        out_specs=(VMEM, VMEM),
        compiler_params=grant(16),
        cost_estimate=pl.CostEstimate(
            flops=12 * n * D * UNITS, transcendentals=n * UNITS, bytes_accessed=4 * n * D + 6 * D * UNITS
        ),
        name="expert_terms",
    )(group, rows, pair_slice, down_slice)


def weight_kernel(*refs):
    u, parts = UNITS, len(refs) // 2
    grad_g, grad_u, grad_d = refs[-3:]
    pairs_of = list(zip(refs[: parts - 1], refs[parts - 1 : -3]))
    for grad, at in ((grad_g, u), (grad_u, 2 * u)):
        total = sum(dot(rows[:, :D], acts[:, at : at + u], 0, 0) for rows, acts in pairs_of)
        grad[0] = total.astype(BF16)
    total = sum(dot(acts[:, :u], rows[:, D : 2 * D], 0, 0) for rows, acts in pairs_of)
    grad_d[0] = total.astype(BF16)


def weight_grads(rows, acts):
    n = sum(r.shape[0] for r in rows)
    return pl.pallas_call(
        weight_kernel,
        out_shape=(
            jax.ShapeDtypeStruct((1, D, UNITS), BF16),
            jax.ShapeDtypeStruct((1, D, UNITS), BF16),
            jax.ShapeDtypeStruct((1, UNITS, D), BF16),
        ),
        in_specs=[VMEM] * (len(rows) + len(acts)),
        out_specs=(VMEM,) * 3,
        compiler_params=grant(8),
        cost_estimate=pl.CostEstimate(
            flops=6 * n * D * UNITS, transcendentals=0, bytes_accessed=4 * n * D + 6 * D * UNITS
        ),
        name="weight_grads",
    )(*rows, *acts)


def last_kernel(own, one, two, three, out):
    x, y = lax.axis_index(("x_hi", "x_lo")), lax.axis_index("y")
    place = jnp.where(lax.axis_index("core") == 0, x, y).astype(jnp.int32)
    for k, d in enumerate((0,) + ORDER):
        at = slice(k * NZ, (k + 1) * NZ)
        total = own[at] + one[at].astype(F32) + two[at].astype(F32) + three[at].astype(F32)
        first = lax.rem(place + d, RING) * NZ
        for i in range(NZ):
            row = total[i : i + 1]
            out[first + i] = jnp.concatenate([row[:, :D], row[:, D:]], axis=0).astype(BF16)


def summed_pairs(own, parts):
    return pl.pallas_call(
        last_kernel,
        out_shape=jax.ShapeDtypeStruct((PLANE, 2, D), BF16),
        in_specs=[VMEM] * 4,
        out_specs=VMEM,
        compiler_params=grant(2),
        name="summed_pairs",
    )(own, *parts)


def on_device(tokens, cotangent, routes, gate_weights, w_gate, w_up, w_down):
    group = lax.axis_index(EP).astype(jnp.int32).reshape(1)
    with jax.named_scope("gather_z"):
        rows = exchanged(copies_of_row(tokens, cotangent, routes, gate_weights), "z")
        rows = jnp.concatenate([rows[:, 0, :D], rows[:, 1, :D], rows[:, 0, D:]], axis=1)
    with jax.named_scope("gather_light"):
        got = {d: fetch(rows, "light", d) for d in ISSUE}
        rows = jnp.concatenate([rows] + [got[d] for d in ORDER], axis=0)
    with jax.named_scope("gather_heavy"):
        got = {d: fetch(rows, "heavy", d) for d in ISSUE}
    with jax.named_scope("gather_core"):
        own, got[2], gate_slice = lax.optimization_barrier((rows, got[2], w_gate[0]))
        slices = (jnp.concatenate([gate_slice, w_up[0]], axis=1), w_down[0])
        near_one = jnp.concatenate([own, got[2]], axis=0)
        far_one = jnp.concatenate([swapped(own), swapped(got[2])], axis=0)
    with jax.named_scope("experts"):
        near_terms_one, near_acts_one = expert_terms(group, near_one, *slices, F32)
        terms_one, acts_one = expert_terms(group, far_one, *slices, BF16)
        other_one = swapped(terms_one)
        near_terms_one, _, got[1], got[3] = lax.optimization_barrier(
            (near_terms_one, terms_one, got[1], got[3])
        )
        near_two = jnp.concatenate([got[1], got[3]], axis=0)
        far_two = jnp.concatenate([swapped(got[1]), swapped(got[3])], axis=0)
        terms_two, acts_two = expert_terms(group, far_two, *slices, BF16)
        other_two = swapped(terms_two)
        near_terms_two, near_acts_two = expert_terms(group, near_two, *slices, F32)
    with jax.named_scope("weights"):
        rows = (far_one, far_two, near_one, near_two)
        grads = weight_grads(rows, (acts_one, acts_two, near_acts_one, near_acts_two))
    with jax.named_scope("reduce_heavy"):
        one = near_terms_one + other_one.astype(F32)
        two = near_terms_two + other_two.astype(F32)
        send = {1: two[:PLANE], 2: one[PLANE:], 3: two[PLANE:]}
        got = {d: give(send[d].astype(BF16), "heavy", d) for d in ISSUE}
        got = [got[d] for d in ORDER]
        *got, grad_g, grad_u, grad_d = lax.optimization_barrier((*got, *grads))
    with jax.named_scope("reduce_plane"):
        got = scattered(summed_pairs(one[:PLANE], got))
        total = sum(got[i].astype(F32) for i in range(PLANE)).astype(BF16)
    return total[:1], total[1:], grad_g, grad_u, grad_d


def solution(mesh):
    fine = Mesh(mesh.devices.reshape(NX_HI, NCORE, NY, NX_LO, NZ), AXES)
    rows, columns, units = P(EP + TP, None), P(EP, None, TP), P(EP, TP, None)
    return jax.shard_map(
        on_device,
        mesh=fine,
        in_specs=(rows, rows, rows, rows, columns, columns, units),
        out_specs=(rows, rows, columns, columns, units),
        check_vma=False,
    )
```

```python
import jax
import jax.numpy as jnp
from jax import lax
from jax.experimental import pallas as pl
from jax.experimental.pallas import tpu as pltpu
from jax.sharding import Mesh, PartitionSpec as P

NX_HI, NCORE, NY, NX_LO, NZ, RING, PLANE = 2, 2, 4, 2, 8, 4, 32
AXES = ("x_hi", "core", "y", "x_lo", "z")
EP, TP = ("x_hi", "core"), ("y", "x_lo", "z")
D, PAD, UNITS = 3072, 128, 128
F32, BF16 = jnp.float32, jnp.bfloat16
VMEM = pl.BlockSpec(memory_space=pltpu.VMEM)
SMEM = pl.BlockSpec(memory_space=pltpu.SMEM)
ORDER, ISSUE = (2, 1, 3), (3, 1, 2)


def grant(mebibytes):
    return pltpu.CompilerParams(vmem_limit_bytes=mebibytes << 20)


def flat(x, core, y, z):
    return (((x // 2) * NCORE + core) * NY + y) * NX_LO * NZ + (x % 2) * NZ + z


def pairs(stage, d):
    out = []
    for x in range(RING):
        for core in range(NCORE):
            for y in range(RING):
                along_x = (stage == "light") == (core == 0)
                tx, ty = ((x + d) % RING, y) if along_x else (x, (y + d) % RING)
                out += [(flat(x, core, y, z), flat(tx, core, ty, z)) for z in range(NZ)]
    return out


def give(value, stage, d):
    return lax.ppermute(value, AXES, pairs(stage, d))


def fetch(value, stage, d):
    return lax.ppermute(value, AXES, pairs(stage, -d))


def swapped(value):
    return lax.ppermute(value, "core", [(0, 1), (1, 0)])


def exchanged(value, axis):
    return lax.all_to_all(value, axis, 0, 0, tiled=True)


def planes():
    along_x = [[flat(x, 0, y, z) for x in range(RING) for z in range(NZ)] for y in range(RING)]
    along_y = [[flat(x, 1, y, z) for y in range(RING) for z in range(NZ)] for x in range(RING)]
    return along_x + along_y


def scattered(value):
    return lax.all_to_all(value, AXES, 0, 0, axis_index_groups=planes(), tiled=True)


def dot(left, right, left_dim, right_dim):
    return lax.dot_general(
        left, right, (((left_dim,), (right_dim,)), ((), ())), preferred_element_type=F32
    )


def row_kernel(tokens, cotangent, routes, weights, out):
    lane = lax.broadcasted_iota(jnp.int32, (1, PAD), 1)
    r, w = routes[...], weights[...].astype(F32)
    gates = jnp.where(r[:, :1] == lane, w[:, :1], 0.0) + jnp.where(r[:, 1:] == lane, w[:, 1:], 0.0)
    first = jnp.concatenate([tokens[...].astype(F32), gates], axis=1)
    second = jnp.concatenate([cotangent[...].astype(F32), jnp.zeros((1, PAD), F32)], axis=1)
    both = jnp.concatenate([first, second], axis=0).astype(BF16)
    for i in range(NZ):
        out[i] = both


def copies_of_row(tokens, cotangent, routes, gate_weights):
    return pl.pallas_call(
        row_kernel,
        out_shape=jax.ShapeDtypeStruct((NZ, 2, D + PAD), BF16),
        out_specs=VMEM,
        name="copies_of_row",
    )(tokens, cotangent, routes, gate_weights)


def expert_kernel(group, rows, pair_slice, down_slice, terms, acts):
    lane = lax.broadcasted_iota(jnp.int32, (rows.shape[0], PAD), 1)
    gates = jnp.where(lane == group[0], rows[:, 2 * D :].astype(F32), 0.0)
    column = jnp.sum(gates, axis=1, keepdims=True)
    x, cot = rows[:, :D], rows[:, D : 2 * D]
    pre = dot(x, pair_slice[...], 1, 0)
    gate_pre, up_pre = pre[:, :UNITS], pre[:, UNITS:]
    grad_act = dot(cot, down_slice[...], 1, 1) * column
    sigmoid = jax.nn.sigmoid(gate_pre)
    silu = gate_pre * sigmoid
    hidden = (silu * up_pre * column).astype(BF16)
    grad_gpre = (grad_act * up_pre * (sigmoid * (1.0 + gate_pre * (1.0 - sigmoid)))).astype(BF16)
    grad_upre = (grad_act * silu).astype(BF16)
    acts[:, :UNITS] = hidden
    acts[:, UNITS : 2 * UNITS] = grad_gpre
    acts[:, 2 * UNITS :] = grad_upre
    terms[:, :D] = dot(hidden, down_slice[...], 1, 0).astype(terms.dtype)
    grad_rows = dot(acts[:, UNITS:], pair_slice[...], 1, 1)
    terms[:, D:] = grad_rows.astype(terms.dtype)


def expert_terms(group, rows, pair_slice, down_slice, kind):
    n = rows.shape[0]
    return pl.pallas_call(
        expert_kernel,
        out_shape=(
            jax.ShapeDtypeStruct((n, 2 * D), kind),
            jax.ShapeDtypeStruct((n, 3 * UNITS), BF16),
        ),
        in_specs=[SMEM] + [VMEM] * 3,
        out_specs=(VMEM, VMEM),
        compiler_params=grant(16),
        cost_estimate=pl.CostEstimate(
            flops=12 * n * D * UNITS, transcendentals=n * UNITS, bytes_accessed=4 * n * D + 6 * D * UNITS
        ),
        name="expert_terms",
    )(group, rows, pair_slice, down_slice)


def weight_kernel(*refs):
    u, parts = UNITS, len(refs) // 2
    grad_g, grad_u, grad_d = refs[-3:]
    pairs_of = list(zip(refs[: parts - 1], refs[parts - 1 : -3]))
    for grad, at in ((grad_g, u), (grad_u, 2 * u)):
        total = sum(dot(rows[:, :D], acts[:, at : at + u], 0, 0) for rows, acts in pairs_of)
        grad[0] = total.astype(BF16)
    total = sum(dot(acts[:, :u], rows[:, D : 2 * D], 0, 0) for rows, acts in pairs_of)
    grad_d[0] = total.astype(BF16)


def weight_grads(rows, acts):
    n = sum(r.shape[0] for r in rows)
    return pl.pallas_call(
        weight_kernel,
        out_shape=(
            jax.ShapeDtypeStruct((1, D, UNITS), BF16),
            jax.ShapeDtypeStruct((1, D, UNITS), BF16),
            jax.ShapeDtypeStruct((1, UNITS, D), BF16),
        ),
        in_specs=[VMEM] * (len(rows) + len(acts)),
        out_specs=(VMEM,) * 3,
        compiler_params=grant(8),
        cost_estimate=pl.CostEstimate(
            flops=6 * n * D * UNITS, transcendentals=0, bytes_accessed=4 * n * D + 6 * D * UNITS
        ),
        name="weight_grads",
    )(*rows, *acts)


def last_kernel(own, one, two, three, out):
    x, y = lax.axis_index(("x_hi", "x_lo")), lax.axis_index("y")
    place = jnp.where(lax.axis_index("core") == 0, x, y).astype(jnp.int32)
    for k, d in enumerate((0,) + ORDER):
        at = slice(k * NZ, (k + 1) * NZ)
        total = own[at] + one[at].astype(F32) + two[at].astype(F32) + three[at].astype(F32)
        first = lax.rem(place + d, RING) * NZ
        for i in range(NZ):
            row = total[i : i + 1]
            out[first + i] = jnp.concatenate([row[:, :D], row[:, D:]], axis=0).astype(BF16)


def summed_pairs(own, parts):
    return pl.pallas_call(
        last_kernel,
        out_shape=jax.ShapeDtypeStruct((PLANE, 2, D), BF16),
        in_specs=[VMEM] * 4,
        out_specs=VMEM,
        compiler_params=grant(2),
        name="summed_pairs",
    )(own, *parts)


def on_device(tokens, cotangent, routes, gate_weights, w_gate, w_up, w_down):
    group = lax.axis_index(EP).astype(jnp.int32).reshape(1)
    with jax.named_scope("gather_z"):
        rows = exchanged(copies_of_row(tokens, cotangent, routes, gate_weights), "z")
        rows = jnp.concatenate([rows[:, 0, :D], rows[:, 1, :D], rows[:, 0, D:]], axis=1)
    with jax.named_scope("gather_light"):
        got = {d: fetch(rows, "light", d) for d in ISSUE}
        rows = jnp.concatenate([rows] + [got[d] for d in ORDER], axis=0)
    with jax.named_scope("gather_heavy"):
        got = {d: fetch(rows, "heavy", d) for d in ISSUE}
    with jax.named_scope("gather_core"):
        own, got[2], gate_slice = lax.optimization_barrier((rows, got[2], w_gate[0]))
        slices = (jnp.concatenate([gate_slice, w_up[0]], axis=1), w_down[0])
        near_one = jnp.concatenate([own, got[2]], axis=0)
        far_one = jnp.concatenate([swapped(own), swapped(got[2])], axis=0)
    with jax.named_scope("experts"):
        near_terms_one, near_acts_one = expert_terms(group, near_one, *slices, F32)
        near_terms_one, got[1], got[3] = lax.optimization_barrier((near_terms_one, got[1], got[3]))
        near_two = jnp.concatenate([got[1], got[3]], axis=0)
        far_two = jnp.concatenate([swapped(got[1]), swapped(got[3])], axis=0)
        terms_one, acts_one = expert_terms(group, far_one, *slices, BF16)
        other_one = swapped(terms_one)
        _, far_two = lax.optimization_barrier((terms_one, far_two))
        terms_two, acts_two = expert_terms(group, far_two, *slices, BF16)
        other_two = swapped(terms_two)
        one = near_terms_one + other_one.astype(F32)
        _, one, near_two = lax.optimization_barrier((terms_two, one, near_two))
        near_terms_two, near_acts_two = expert_terms(group, near_two, *slices, F32)
    with jax.named_scope("weights"):
        rows = (far_one, far_two, near_one, near_two)
        grads = weight_grads(rows, (acts_one, acts_two, near_acts_one, near_acts_two))
    with jax.named_scope("reduce_heavy"):
        two = near_terms_two + other_two.astype(F32)
        send = {1: two[:PLANE], 2: one[PLANE:], 3: two[PLANE:]}
        got = {d: give(send[d].astype(BF16), "heavy", d) for d in ISSUE}
        got = [got[d] for d in ORDER]
        *got, grad_g, grad_u, grad_d = lax.optimization_barrier((*got, *grads))
    with jax.named_scope("reduce_plane"):
        got = scattered(summed_pairs(one[:PLANE], got))
        total = sum(got[i].astype(F32) for i in range(PLANE)).astype(BF16)
    return total[:1], total[1:], grad_g, grad_u, grad_d


def solution(mesh):
    fine = Mesh(mesh.devices.reshape(NX_HI, NCORE, NY, NX_LO, NZ), AXES)
    rows, columns, units = P(EP + TP, None), P(EP, None, TP), P(EP, TP, None)
    return jax.shard_map(
        on_device,
        mesh=fine,
        in_specs=(rows, rows, rows, rows, columns, columns, units),
        out_specs=(rows, rows, columns, columns, units),
        check_vma=False,
    )
```

```python
import jax
import jax.numpy as jnp
from jax import lax
from jax.experimental import pallas as pl
from jax.experimental.pallas import tpu as pltpu
from jax.sharding import Mesh, PartitionSpec as P

NX_HI, NCORE, NY, NX_LO, NZ, RING, PLANE = 2, 2, 4, 2, 8, 4, 32
AXES = ("x_hi", "core", "y", "x_lo", "z")
EP, TP = ("x_hi", "core"), ("y", "x_lo", "z")
D, PAD, UNITS = 3072, 128, 128
F32, BF16 = jnp.float32, jnp.bfloat16
VMEM = pl.BlockSpec(memory_space=pltpu.VMEM)
SMEM = pl.BlockSpec(memory_space=pltpu.SMEM)
ORDER, ISSUE = (2, 1, 3), (3, 1, 2)


def grant(mebibytes):
    return pltpu.CompilerParams(vmem_limit_bytes=mebibytes << 20)


def flat(x, core, y, z):
    return (((x // 2) * NCORE + core) * NY + y) * NX_LO * NZ + (x % 2) * NZ + z


def pairs(stage, d):
    out = []
    for x in range(RING):
        for core in range(NCORE):
            for y in range(RING):
                along_x = (stage == "light") == (core == 0)
                tx, ty = ((x + d) % RING, y) if along_x else (x, (y + d) % RING)
                out += [(flat(x, core, y, z), flat(tx, core, ty, z)) for z in range(NZ)]
    return out


def give(value, stage, d):
    return lax.ppermute(value, AXES, pairs(stage, d))


def fetch(value, stage, d):
    return lax.ppermute(value, AXES, pairs(stage, -d))


def swapped(value):
    return lax.ppermute(value, "core", [(0, 1), (1, 0)])


def exchanged(value, axis):
    return lax.all_to_all(value, axis, 0, 0, tiled=True)


def planes():
    along_x = [[flat(x, 0, y, z) for x in range(RING) for z in range(NZ)] for y in range(RING)]
    along_y = [[flat(x, 1, y, z) for y in range(RING) for z in range(NZ)] for x in range(RING)]
    return along_x + along_y


def scattered(value):
    return lax.all_to_all(value, AXES, 0, 0, axis_index_groups=planes(), tiled=True)


def dot(left, right, left_dim, right_dim):
    return lax.dot_general(
        left, right, (((left_dim,), (right_dim,)), ((), ())), preferred_element_type=F32
    )


def row_kernel(tokens, cotangent, routes, weights, out):
    lane = lax.broadcasted_iota(jnp.int32, (1, PAD), 1)
    r, w = routes[...], weights[...].astype(F32)
    gates = jnp.where(r[:, :1] == lane, w[:, :1], 0.0) + jnp.where(r[:, 1:] == lane, w[:, 1:], 0.0)
    first = jnp.concatenate([tokens[...].astype(F32), gates], axis=1)
    second = jnp.concatenate([cotangent[...].astype(F32), jnp.zeros((1, PAD), F32)], axis=1)
    both = jnp.concatenate([first, second], axis=0).astype(BF16)
    for i in range(NZ):
        out[i] = both


def copies_of_row(tokens, cotangent, routes, gate_weights):
    return pl.pallas_call(
        row_kernel,
        out_shape=jax.ShapeDtypeStruct((NZ, 2, D + PAD), BF16),
        out_specs=VMEM,
        name="copies_of_row",
    )(tokens, cotangent, routes, gate_weights)


def expert_kernel(group, rows, pair_slice, down_slice, terms, acts):
    lane = lax.broadcasted_iota(jnp.int32, (rows.shape[0], PAD), 1)
    gates = jnp.where(lane == group[0], rows[:, 2 * D :].astype(F32), 0.0)
    column = jnp.sum(gates, axis=1, keepdims=True)
    x, cot = rows[:, :D], rows[:, D : 2 * D]
    pre = dot(x, pair_slice[...], 1, 0)
    gate_pre, up_pre = pre[:, :UNITS], pre[:, UNITS:]
    grad_act = dot(cot, down_slice[...], 1, 1) * column
    sigmoid = jax.nn.sigmoid(gate_pre)
    silu = gate_pre * sigmoid
    hidden = (silu * up_pre * column).astype(BF16)
    grad_gpre = (grad_act * up_pre * (sigmoid * (1.0 + gate_pre * (1.0 - sigmoid)))).astype(BF16)
    grad_upre = (grad_act * silu).astype(BF16)
    acts[:, :UNITS] = hidden
    acts[:, UNITS : 2 * UNITS] = grad_gpre
    acts[:, 2 * UNITS :] = grad_upre
    terms[:, :D] = dot(hidden, down_slice[...], 1, 0).astype(terms.dtype)
    grad_rows = dot(acts[:, UNITS:], pair_slice[...], 1, 1)
    terms[:, D:] = grad_rows.astype(terms.dtype)


def expert_terms(group, rows, pair_slice, down_slice, kind):
    n = rows.shape[0]
    return pl.pallas_call(
        expert_kernel,
        out_shape=(
            jax.ShapeDtypeStruct((n, 2 * D), kind),
            jax.ShapeDtypeStruct((n, 3 * UNITS), BF16),
        ),
        in_specs=[SMEM] + [VMEM] * 3,
        out_specs=(VMEM, VMEM),
        compiler_params=grant(16),
        cost_estimate=pl.CostEstimate(
            flops=12 * n * D * UNITS, transcendentals=n * UNITS, bytes_accessed=4 * n * D + 6 * D * UNITS
        ),
        name="expert_terms",
    )(group, rows, pair_slice, down_slice)


def weight_kernel(*refs):
    u, parts = UNITS, len(refs) // 2
    grad_g, grad_u, grad_d = refs[-3:]
    pairs_of = list(zip(refs[: parts - 1], refs[parts - 1 : -3]))
    for grad, at in ((grad_g, u), (grad_u, 2 * u)):
        total = sum(dot(rows[:, :D], acts[:, at : at + u], 0, 0) for rows, acts in pairs_of)
        grad[0] = total.astype(BF16)
    total = sum(dot(acts[:, :u], rows[:, D : 2 * D], 0, 0) for rows, acts in pairs_of)
    grad_d[0] = total.astype(BF16)


def weight_grads(rows, acts):
    n = sum(r.shape[0] for r in rows)
    return pl.pallas_call(
        weight_kernel,
        out_shape=(
            jax.ShapeDtypeStruct((1, D, UNITS), BF16),
            jax.ShapeDtypeStruct((1, D, UNITS), BF16),
            jax.ShapeDtypeStruct((1, UNITS, D), BF16),
        ),
        in_specs=[VMEM] * (len(rows) + len(acts)),
        out_specs=(VMEM,) * 3,
        compiler_params=grant(8),
        cost_estimate=pl.CostEstimate(
            flops=6 * n * D * UNITS, transcendentals=0, bytes_accessed=4 * n * D + 6 * D * UNITS
        ),
        name="weight_grads",
    )(*rows, *acts)


def last_kernel(own, one, two, three, out):
    x, y = lax.axis_index(("x_hi", "x_lo")), lax.axis_index("y")
    place = jnp.where(lax.axis_index("core") == 0, x, y).astype(jnp.int32)
    for k, d in enumerate((0,) + ORDER):
        at = slice(k * NZ, (k + 1) * NZ)
        total = own[at] + one[at].astype(F32) + two[at].astype(F32) + three[at].astype(F32)
        first = lax.rem(place + d, RING) * NZ
        for i in range(NZ):
            row = total[i : i + 1]
            out[first + i] = jnp.concatenate([row[:, :D], row[:, D:]], axis=0).astype(BF16)


def summed_pairs(own, parts):
    return pl.pallas_call(
        last_kernel,
        out_shape=jax.ShapeDtypeStruct((PLANE, 2, D), BF16),
        in_specs=[VMEM] * 4,
        out_specs=VMEM,
        compiler_params=grant(2),
        name="summed_pairs",
    )(own, *parts)


def on_device(tokens, cotangent, routes, gate_weights, w_gate, w_up, w_down):
    group = lax.axis_index(EP).astype(jnp.int32).reshape(1)
    with jax.named_scope("gather_z"):
        rows = exchanged(copies_of_row(tokens, cotangent, routes, gate_weights), "z")
        rows = jnp.concatenate([rows[:, 0, :D], rows[:, 1, :D], rows[:, 0, D:]], axis=1)
    with jax.named_scope("gather_light"):
        got = {d: fetch(rows, "light", d) for d in ISSUE}
        rows = jnp.concatenate([rows] + [got[d] for d in ORDER], axis=0)
    with jax.named_scope("gather_heavy"):
        got = {d: fetch(rows, "heavy", d) for d in ISSUE}
    with jax.named_scope("gather_core"):
        own, got[2], gate_slice = lax.optimization_barrier((rows, got[2], w_gate[0]))
        slices = (jnp.concatenate([gate_slice, w_up[0]], axis=1), w_down[0])
        near_one = jnp.concatenate([own, got[2]], axis=0)
        far_one = jnp.concatenate([swapped(own), swapped(got[2])], axis=0)
    with jax.named_scope("experts"):
        near_terms_one, near_acts_one = expert_terms(group, near_one, *slices, F32)
        near_terms_one, got[1], got[3] = lax.optimization_barrier((near_terms_one, got[1], got[3]))
        near_two = jnp.concatenate([got[1], got[3]], axis=0)
        far_two = jnp.concatenate([swapped(got[1]), swapped(got[3])], axis=0)
        terms_one, acts_one = expert_terms(group, far_one, *slices, BF16)
        other_one = swapped(terms_one)
        _, far_two = lax.optimization_barrier((terms_one, far_two))
        last = jnp.concatenate([far_two, near_two], axis=0)
        last_terms, last_acts = expert_terms(group, last, *slices, F32)
        other_two = swapped(last_terms[: 2 * PLANE].astype(BF16))
        near_terms_two = last_terms[2 * PLANE :]
        one = near_terms_one + other_one.astype(F32)
    with jax.named_scope("weights"):
        grads = weight_grads((far_one, near_one, last), (acts_one, near_acts_one, last_acts))
    with jax.named_scope("reduce_heavy"):
        two = near_terms_two + other_two.astype(F32)
        send = {1: two[:PLANE], 2: one[PLANE:], 3: two[PLANE:]}
        got = {d: give(send[d].astype(BF16), "heavy", d) for d in ISSUE}
        got = [got[d] for d in ORDER]
        *got, grad_g, grad_u, grad_d = lax.optimization_barrier((*got, *grads))
    with jax.named_scope("reduce_plane"):
        got = scattered(summed_pairs(one[:PLANE], got))
        total = sum(got[i].astype(F32) for i in range(PLANE)).astype(BF16)
    return total[:1], total[1:], grad_g, grad_u, grad_d


def solution(mesh):
    fine = Mesh(mesh.devices.reshape(NX_HI, NCORE, NY, NX_LO, NZ), AXES)
    rows, columns, units = P(EP + TP, None), P(EP, None, TP), P(EP, TP, None)
    return jax.shard_map(
        on_device,
        mesh=fine,
        in_specs=(rows, rows, rows, rows, columns, columns, units),
        out_specs=(rows, rows, columns, columns, units),
        check_vma=False,
    )
```
